256 devices in a mesh: sub: 64 (over z, x, core), col: 4 (over y).
Axes of the slice: x: 4, y: 4, z: 8, core: 2. Of those that a mesh axis runs over, the one named last changes fastest.
Arguments:
- adjoint_source: float32 [64, 98304], P('col', 'sub'), may hold values from -4 to 4
- start_field: float32 [64, 98304], P('col', 'sub'), may hold values from -3 to 3
- row_diagonal: float32 [98304], P('sub'), may hold values from 2 to 4
- row_values: float32 [26, 98304], P(None, 'sub'), may hold values from -0.6 to 0.6
- row_columns: int32 [26, 98304], P(None, 'sub'), may hold values from 0 to 2047
- weight_code: int32 [131072], P('sub'), may hold values from 0 to 3
- slot_count: int32 [64, 4], P('sub'), may hold values from 0 to 128, as said below
- slot_rows: int32 [64, 4, 128], P('sub'), may hold values from 0 to 1535, as said below
- local_inverse: float32 [131072, 2048], P(('sub', 'col')), may hold values from -0.006629126 to 0.60662913
- coarse_modes: float32 [4, 98304], P(None, 'sub'), may hold values from -0.15309311 to 0.15309311
- coarse_inverse: float32 [256, 256], P('sub'), may hold values from -0.028125 to 0.628125
Outputs:
- adjoint: float32 [64, 98304], P('col', 'sub')
The draws below stay inside these ranges and needn't reach their ends.
Inputs may be any that keep to these rules, and one draw needn't show every extreme that they name: slot_count[s, d] counts the live slots that subdomain s takes from subdomain s - 2, s - 1, s + 1, s + 2 for d = 0, 1, 2, 3; it is zero where that subdomain does not exist, and some entry equals 128 in every draw. `slot_rows`: the entries of one subdomain and direction are distinct.
All inputs are finite; a program needn't handle non-finite values.
Results may differ from the reference program's by a relative error of at most 0.00016.
Values sent between devices are 32-bit elements; how exact they have to be, the bound alone decides.
No kernel may reach another device: no remote copies, remote signals or barrier semaphores. Data moves between devices by JAX's collectives and lax.ppermute only.
A program may use at most 128 MiB of HBM per device.

```python
import math
import jax
import jax.numpy as jnp
from jax import lax

OWN = 1536
MAXR = 128
TERMS = 26
MODES = 4
ITERS = 3
EXT = 2048
SUBS = 64
NCOL = 64
NTOT = 98304
NEXT = 131072
COARSE = 256


def draw_adjoint_source(key, part):
    return jnp.clip(jax.random.normal(key, (NCOL, NTOT), jnp.float32), -4.0, 4.0)


def inverse_draw(key, blocks, order, off_scale):
    key_diag, key_off = jax.random.split(jax.random.fold_in(key, 11))
    half_width = off_scale / order ** 0.5
    spread = jax.random.uniform(key_off, (blocks * order, order), jnp.float32, -half_width, half_width)
    diagonal = jnp.exp(jax.random.uniform(key_diag, (blocks * order,), jnp.float32, math.log(0.3), math.log(0.6)))
    row_index = jnp.arange(blocks * order, dtype=jnp.int32) % order
    column_index = jnp.arange(order, dtype=jnp.int32)
    return spread + jnp.where(row_index[:, None] == column_index[None, :], diagonal[:, None], 0.0)


def draw_local_inverse(key, part):
    return inverse_draw(key, SUBS, EXT, 0.3)


def draw_coarse_inverse(key, part):
    return inverse_draw(key, 1, COARSE, 0.45)


def draw_slot_count(key, part):
    key_one, key_two, key_three = jax.random.split(jax.random.fold_in(key, 23), 3)
    source = jnp.arange(SUBS, dtype=jnp.int32)[:, None] + jnp.array([-2, -1, 1, 2], dtype=jnp.int32)[None, :]
    inside = (source >= 0) & (source < SUBS)
    amount = jax.random.randint(key_one, (SUBS, 4), MAXR // 4, MAXR + 1)
    present = jax.random.randint(key_two, (SUBS, 4), 0, 2)
    far_mask = jnp.array([1, 0, 0, 1], dtype=jnp.int32)[None, :]
    amount = amount * jnp.where(far_mask == 1, present, 1)
    amount = jnp.where(inside, amount, 0)
    chosen = jax.random.randint(key_three, (), 0, SUBS - 1)
    amount = amount.at[chosen, 2].set(MAXR)
    return amount.astype(jnp.int32)


def draw_slot_rows(key, part):
    subkeys = jax.random.split(jax.random.fold_in(key, 31), SUBS * 4)

    def one_list(single):
        return jax.random.permutation(single, OWN)[:MAXR]
    picked = jax.vmap(one_list)(subkeys)
    return picked.reshape(SUBS, 4, MAXR).astype(jnp.int32)


def with_ends(entries, rng, low, high):
    longest = entries.shape.index(max(entries.shape))
    spots = []
    for shift in (0, 1):
        where = [jax.random.randint(jax.random.fold_in(rng, axis), (), 0, length) for axis, length in enumerate(entries.shape)]
        where[longest] = (where[longest] + shift) % entries.shape[longest]
        spots.append(tuple(where))
    return entries.at[spots[0]].set(low).at[spots[1]].set(high)


def levels(stream_key, shape, cuts, least, top_value):
    loudness, own = 1.0, jax.random.fold_in(stream_key, 6)
    for position, blocks in cuts:
        draws = jnp.exp(jax.random.uniform(jax.random.fold_in(own, position), (blocks,), jnp.float32, least / len(cuts), top_value / len(cuts)))
        loudness = loudness * jnp.repeat(draws, shape[position] // blocks).reshape([-1 if axis == position else 1 for axis in range(len(shape))])
    return loudness


def centred(stream_key, extent, deviation, bound, shards=(), held_as=jnp.bfloat16):
    drawn = jax.random.normal(stream_key, extent, jnp.float32) * deviation
    if len(shards) > 0:
        drawn = levels(stream_key, extent, shards, -0.22, 0.18) * drawn
    return jnp.clip(drawn, min=-bound, max=bound).astype(held_as)


def setup_inputs(seed: int = 0) -> dict:
    key_list = jax.random.split(jax.random.key(seed), 12)
    adjoint_source = draw_adjoint_source(jax.random.fold_in(key_list[11], 71), 0)
    start_field = centred(key_list[1], (NCOL, NTOT), 0.5, 3.0, ((0, 4), (1, 64)), jnp.float32)
    row_diagonal = jnp.clip(jnp.exp(math.log(4.0) - 0.6931472 * jax.random.uniform(key_list[2], (NTOT,), jnp.float32) ** levels(key_list[2], (NTOT,), ((0, 64),), -0.2, 0.2)), 2.0, 4.0)
    row_values = centred(key_list[3], (TERMS, NTOT), 0.15, 0.6, ((1, 64),), jnp.float32)
    row_columns = with_ends(jax.random.randint(key_list[4], (TERMS, NTOT), 0, EXT), jax.random.fold_in(key_list[4], 1), 0, EXT - 1).astype(jnp.int32)
    weight_code = with_ends(jax.random.randint(key_list[5], (NEXT,), 0, 4), jax.random.fold_in(key_list[5], 1), 0, 3).astype(jnp.int32)
    slot_count = draw_slot_count(jax.random.fold_in(key_list[11], 71), 0)
    slot_rows = draw_slot_rows(jax.random.fold_in(key_list[11], 71), 0)
    local_inverse = draw_local_inverse(jax.random.fold_in(key_list[11], 71), 0)
    coarse_modes = centred(key_list[9], (MODES, NTOT), (1.3 / OWN ** 0.5), 0.15309311, ((1, 64),), jnp.float32)
    coarse_inverse = draw_coarse_inverse(jax.random.fold_in(key_list[11], 71), 0)
    return dict(adjoint_source=adjoint_source, start_field=start_field, row_diagonal=row_diagonal, row_values=row_values, row_columns=row_columns, weight_code=weight_code, slot_count=slot_count, slot_rows=slot_rows, local_inverse=local_inverse, coarse_modes=coarse_modes, coarse_inverse=coarse_inverse)


direction_steps = (-2, -1, 1, 2)
damping = 0.7
highest = lax.Precision.HIGHEST


def extend(values, slot_count, slot_rows):
    index_list = jnp.arange(SUBS, dtype=jnp.int32)
    slot_index = jnp.arange(MAXR, dtype=jnp.int32)
    pieces = [values]
    for number, offset in enumerate(direction_steps):
        source = jnp.clip(index_list + offset, 0, SUBS - 1)
        shifted = values[:, source, :]
        wanted = jnp.broadcast_to(slot_rows[None, :, number, :], (values.shape[0], SUBS, MAXR))
        taken_rows = jnp.take_along_axis(shifted, wanted, axis=2)
        live_mask = (slot_index[None, :] < slot_count[:, number:number + 1]).astype(values.dtype)
        pieces.append(taken_rows * live_mask[None])
    return jnp.concatenate(pieces, axis=2)


def reference(adjoint_source, start_field, row_diagonal, row_values, row_columns, weight_code, slot_count, slot_rows, local_inverse, coarse_modes, coarse_inverse):
    columns = adjoint_source.shape[0]
    source_grid = adjoint_source.reshape(columns, SUBS, OWN)
    field_grid = start_field.reshape(columns, SUBS, OWN)
    diagonal_grid = row_diagonal.reshape(SUBS, OWN)
    values_grid = row_values.reshape(TERMS, SUBS, OWN)
    indices_grid = row_columns.reshape(TERMS, SUBS, OWN)
    weights = 1.0 / (1.0 + weight_code.reshape(SUBS, EXT).astype(jnp.float32))
    inverse_grid = local_inverse.reshape(SUBS, EXT, EXT)
    modes_grid = coarse_modes.reshape(MODES, SUBS, OWN)
    slot_index = jnp.arange(MAXR, dtype=jnp.int32)
    index_list = jnp.arange(SUBS, dtype=jnp.int32)

    def solve_one(operands):
        block_inverse, block_rhs = operands
        return lax.dot_general(block_rhs, block_inverse, (((1,), (1,)), ((), ())), precision=highest)

    for iteration in range(ITERS):
        extended = extend(field_grid, slot_count, slot_rows)

        def add_term(running, term_pair):
            term_values, term_columns = term_pair
            wanted = jnp.broadcast_to(term_columns[None], running.shape)
            taken_rows = jnp.take_along_axis(extended, wanted, axis=2)
            return running + term_values[None] * taken_rows, None

        residual_sum, unused = lax.scan(add_term, jnp.zeros_like(field_grid), (values_grid, indices_grid))
        residual = source_grid - diagonal_grid[None] * field_grid - residual_sum
        weighted = extend(residual, slot_count, slot_rows) * weights[None]
        solved = lax.map(solve_one, (inverse_grid, jnp.transpose(weighted, (1, 0, 2))))
        solved = jnp.transpose(solved, (1, 0, 2))
        correction = solved[:, :, :OWN]
        for number, offset in enumerate(direction_steps):
            live_mask = (slot_index[None, :] < slot_count[:, number:number + 1]).astype(field_grid.dtype)
            slot_values = solved[:, :, OWN + number * MAXR:OWN + (number + 1) * MAXR] * live_mask[None]
            target = jnp.broadcast_to(jnp.clip(index_list + offset, 0, SUBS - 1)[:, None], (SUBS, MAXR))
            correction = correction.at[:, target, slot_rows[:, number, :]].add(slot_values)
        coarse_rhs = jnp.einsum("csi,msi->csm", residual, modes_grid, precision=highest).reshape(columns, COARSE)
        coarse = lax.dot_general(coarse_rhs, coarse_inverse, (((1,), (1,)), ((), ())), precision=highest)
        coarse = coarse.reshape(columns, SUBS, MODES)
        lifted = jnp.einsum("csm,msi->csi", coarse, modes_grid, precision=highest)
        field_grid = field_grid + damping * (correction + lifted)
    return field_grid.reshape(columns, SUBS * OWN)
```

```python
import functools
import jax
import jax.numpy as jnp
from jax import lax
from jax.experimental import pallas as pl
from jax.experimental.pallas import tpu as pltpu
from jax.sharding import PartitionSpec as P

ITERS = 3
OWN = 1536
EXT = 2048
SLOT = 128
QUART = 384
BLOCK = 512
TERMS = 26
MODES = 4
SUBS = 64
TEAM = 4
COLS = 16
ALLC = 64

direction_steps = (-2, -1, 1, 2)
damping = 0.7
highest = lax.Precision.HIGHEST
f32 = jnp.float32
bf16 = jnp.bfloat16
contract_last = (((1,), (1,)), ((), ()))
contract_first = (((0,), (0,)), ((), ()))


def chunk_of(block, place):
    if block < 3 and place < 3:
        return 4 * block + place
    if place == 3:
        return 12 + block
    return 4 * place + 3


def dyn_chunk(member, place):
    return jnp.where(member < 3, 4 * member + place, 4 * place + 3)


def source_of(member, step):
    return lax.rem(member - step + TEAM, TEAM)


def split(x):
    high = x.astype(bf16)
    low = (x - high.astype(f32)).astype(bf16)
    return high, low


def dot(a, b):
    return jnp.dot(a, b, preferred_element_type=f32)


def dot3(x, w_high, w_low):
    rows = x.shape[0]
    high, low = split(x)
    both = dot(jnp.concatenate([high, low], axis=0), w_high)
    return both[:rows] + both[rows:] + dot(high, w_low)


def dot2(x, ones):
    rows = x.shape[0]
    high, low = split(x)
    both = dot(jnp.concatenate([high, low], axis=0), ones)
    return both[:rows] + both[rows:]


def setup_kernel(x0, x1, x2, x3, list_row, modes, inverse, lam, bvec, pick, slots, modes_out, inv_out, bscr):
    me = lax.axis_index("col")
    wanted = list_row[...] - 1
    for step, x in enumerate((x0, x1, x2, x3)):
        rows = pl.ds(pl.multiple_of(COLS * source_of(me, step), COLS), COLS)
        for b in range(4):
            for j in range(3):
                n = 128 * chunk_of(b, j)
                lam[b, rows, 128 * j : 128 * j + 128] = x[0:COLS, n : n + 128]
                bscr[b, rows, 128 * j : 128 * j + 128] = x[COLS : 2 * COLS, n : n + 128]
    for j in range(3):
        bvec[:, 128 * j : 128 * j + 128] = bscr[me, :, 128 * j : 128 * j + 128]
    send = jnp.zeros((ALLC, SLOT), f32)
    bsel = jnp.zeros((ALLC, SLOT), f32)
    modes_out[...] = jnp.zeros(modes_out.shape, f32)
    for b in range(4):
        for j in range(3):
            n = 128 * chunk_of(b, j)
            spot = lax.broadcasted_iota(jnp.int32, (128, SLOT), 0) + n
            pick[b, 128 * j : 128 * j + 128, :] = (spot == wanted).astype(f32).astype(bf16)
            modes_out[b, 0:MODES, 128 * j : 128 * j + 128] = modes[:, n : n + 128]
        ones = pick[b].astype(f32)
        send = send + jnp.dot(lam[b], ones, precision=highest, preferred_element_type=f32)
        bsel = bsel + jnp.dot(bscr[b], ones, precision=highest, preferred_element_type=f32)
    slots[...] = send
    bvec[:, QUART:] = bsel
    width = SUBS * MODES
    at = lax.broadcasted_iota(jnp.int32, (width, SUBS * 8), 0)
    to = lax.broadcasted_iota(jnp.int32, (width, SUBS * 8), 1)
    spread = jnp.logical_and(at // MODES == to // 8, lax.rem(at, MODES) == lax.rem(to, 8)).astype(f32)
    inv_out[...] = jnp.zeros(inv_out.shape, f32)
    inv_out[0:MODES, :] = jnp.dot(inverse[...], spread, precision=highest, preferred_element_type=f32)


def lists_kernel(l0, l1, l2, l3, spread):
    me = lax.axis_index("col")
    for step, column in enumerate((l0, l1, l2, l3)):
        at = pl.multiple_of(SLOT * source_of(me, step), SLOT)
        wanted = column[...] - 1
        for b in range(4):
            for j in range(3):
                n = 128 * chunk_of(b, j)
                spot = lax.broadcasted_iota(jnp.int32, (SLOT, 128), 1) + n
                spread[b, pl.ds(at, SLOT), 128 * j : 128 * j + 128] = (spot == wanted).astype(f32).astype(bf16)


def operator_kernel(values, columns, diagonal, list_row, pick, high, low, val, col):
    me = lax.axis_index("col")
    for j in range(3):
        at = pl.ds(pl.multiple_of(128 * dyn_chunk(me, j), 128), 128)
        to = slice(128 * j, 128 * j + 128)
        val[0:TERMS, to] = values[:, at]
        col[0:TERMS, to] = columns[:, at]
        val[TERMS : TERMS + 1, to] = diagonal[:, at]
        col[TERMS : TERMS + 1, to] = lax.broadcasted_iota(jnp.int32, (1, 128), 1) + 128 * dyn_chunk(me, j)
    vsel = jnp.zeros((TERMS, SLOT), f32)
    csel = jnp.zeros((TERMS, SLOT), f32)
    dsel = jnp.zeros((8, SLOT), f32)
    for b in range(4):
        for j in range(3):
            n = 128 * chunk_of(b, j)
            ones = pick[b, 128 * j : 128 * j + 128, :].astype(f32)
            vsel = vsel + jnp.dot(values[:, n : n + 128], ones, precision=highest, preferred_element_type=f32)
            csel = csel + jnp.dot(columns[:, n : n + 128].astype(f32), ones, precision=highest, preferred_element_type=f32)
            diag = jnp.broadcast_to(diagonal[:, n : n + 128], (8, 128))
            dsel = dsel + jnp.dot(diag, ones, precision=highest, preferred_element_type=f32)
    val[0:TERMS, QUART:] = vsel
    col[0:TERMS, QUART:] = (csel + 0.5).astype(jnp.int32)
    val[TERMS : TERMS + 1, QUART:] = dsel[0:1]
    col[TERMS : TERMS + 1, QUART:] = list_row[...] - 1

    for b in range(4):
        for j in range(4):
            n = 128 * chunk_of(b, j)

            def body(q, carry, n=n, b=b, j=j):
                at = pl.multiple_of(q * 32, 32)
                spot = lax.broadcasted_iota(jnp.int32, (32, 128), 0) + (n + at)
                for lane in range(4):
                    to = slice(128 * lane, 128 * lane + 128)
                    total = jnp.zeros((32, 128), f32)
                    for term in range(TERMS + 1):
                        total = total + jnp.where(spot == col[term : term + 1, to], val[term : term + 1, to], 0.0)
                    first, second = split(total)
                    high[b, pl.ds(128 * j + at, 32), to] = first
                    low[b, pl.ds(128 * j + at, 32), to] = second
                return carry

            lax.fori_loop(0, 4, body, 0)


def inverse_kernel(mine, r1, r2, r3, code, high, low):
    me = lax.axis_index("col")
    last = me == 3
    b = pl.program_id(0)
    for j in range(4):
        lanes = slice(128 * j, 128 * j + 128)
        weight = 1.0 / (1.0 + code[:, lanes].astype(f32))
        for place in range(4):
            rows = slice(128 * place, 128 * place + 128)
            own = mine[rows, lanes]
            if place < 3:
                other = (r3, r2, r1)[place][:, lanes]
                tile = jnp.where(last, other, own)
            else:
                got = jnp.where(me == 0, r1[:, lanes], jnp.where(me == 1, r2[:, lanes], r3[:, lanes]))
                tile = jnp.where(last, own, got)
            first, second = split((tile * weight).T)
            chunk_high = first
            if j < 3:
                @pl.when(b < 3)
                def _():
                    high[pl.ds(b, 1), lanes, rows] = first[None]
                    low[pl.ds(b, 1), lanes, rows] = second[None]

                @pl.when(b == 3)
                def _():
                    high[pl.ds(j, 1), 384:512, rows] = first[None]
                    low[pl.ds(j, 1), 384:512, rows] = second[None]
            else:
                @pl.when(b < 3)
                def _():
                    at = pl.ds(pl.multiple_of(128 * b, 128), 128)
                    high[3:4, at, rows] = first[None]
                    low[3:4, at, rows] = second[None]

                @pl.when(b == 3)
                def _():
                    high[3:4, 384:512, rows] = first[None]
                    low[3:4, 384:512, rows] = second[None]


def residual_kernel(lam, s0, s1, s2, s3, high, low, bvec, quarter, slots, scr):
    me = lax.axis_index("col")
    for step, s in enumerate((s0, s1, s2, s3)):
        scr[source_of(me, step)] = s[...]
    total = jnp.zeros((ALLC, BLOCK), f32)
    for b in range(4):
        total = total + dot3(jnp.concatenate([lam[b], scr[b]], axis=1), high[b], low[b])
    out = bvec[...] - total
    quarter[...] = out[:, :QUART]
    slots[...] = out[:, QUART:]


def solve_kernel(x0, x1, x2, x3, high, low, modes, quarter, slots, message, scr):
    me = lax.axis_index("col")
    for step, x in enumerate((x0, x1, x2, x3)):
        scr[source_of(me, step)] = x[...]
    total = jnp.zeros((ALLC, BLOCK), f32)
    rhs = jnp.zeros((8, ALLC), f32)
    for b in range(4):
        x = scr[b]
        total = total + dot3(x, high[b], low[b])
        rhs = rhs + lax.dot_general(
            modes[b], x[:, :QUART], contract_last, precision=highest, preferred_element_type=f32
        )
    quarter[...] = total[:, :QUART]
    slots[...] = total[:, QUART:]
    padded = jnp.concatenate([rhs, jnp.zeros((8, 128 - ALLC), f32)], axis=1)
    message[...] = jnp.broadcast_to(padded[None], message.shape)


def new_field(refs, lam, spread, modes, inverse, coarse_rhs, scr):
    me = lax.axis_index("col")
    for step, x in enumerate(refs):
        scr[source_of(me, step)] = x[...]
    back = jnp.concatenate([scr[b, :, QUART:] for b in range(4)], axis=1)
    coarse = jnp.dot(inverse[...], coarse_rhs[...], precision=highest, preferred_element_type=f32)
    coarse = coarse.T[:ALLC]
    result = []
    for b in range(4):
        lifted = jnp.dot(coarse, modes[b], precision=highest, preferred_element_type=f32)
        result.append(lam[b] + damping * (scr[b, :, :QUART] + dot2(back, spread[b]) + lifted))
    return result


def update_kernel(x0, x1, x2, x3, lam, spread, modes, inverse, coarse_rhs, pick, out, slots, scr):
    result = new_field((x0, x1, x2, x3), lam, spread, modes, inverse, coarse_rhs, scr)
    send = jnp.zeros((ALLC, SLOT), f32)
    for b in range(4):
        out[b] = result[b]
        send = send + dot2(result[b], pick[b])
    slots[...] = send


def final_kernel(x0, x1, x2, x3, lam, spread, modes, inverse, coarse_rhs, out, scr, field):
    me = lax.axis_index("col")
    result = new_field((x0, x1, x2, x3), lam, spread, modes, inverse, coarse_rhs, scr)
    rows = pl.ds(pl.multiple_of(COLS * me, COLS), COLS)
    for b in range(4):
        field[b] = result[b]
        for j in range(3):
            n = 128 * chunk_of(b, j)
            out[:, n : n + 128] = field[b, rows, 128 * j : 128 * j + 128]


def call(kernel, outs, scratch, flops, nbytes, *args, limit=32 << 20):
    return pl.pallas_call(
        kernel,
        out_shape=[jax.ShapeDtypeStruct(shape, dtype) for shape, dtype in outs],
        in_specs=[pl.BlockSpec(memory_space=pltpu.VMEM)] * len(args),
        out_specs=[pl.BlockSpec(memory_space=pltpu.VMEM)] * len(outs),
        scratch_shapes=[pltpu.VMEM(shape, dtype) for shape, dtype in scratch],
        compiler_params=pltpu.CompilerParams(vmem_limit_bytes=limit),
        cost_estimate=pl.CostEstimate(flops=flops, bytes_accessed=nbytes, transcendentals=0),
    )(*args)


def team_pass(x, sign):
    pairs = []
    for s in range(SUBS):
        for d, step in enumerate(direction_steps):
            t = s + sign * step
            if 0 <= t < SUBS:
                pairs.append((s * TEAM + d, t * TEAM + d))
    return lax.ppermute(x, ("sub", "col"), pairs)


def team_share(x):
    return [x] + [
        lax.ppermute(x, "col", [(i, (i + step) % TEAM) for i in range(TEAM)]) for step in (1, 2, 3)
    ]


def local(
    adjoint_source,
    start_field,
    row_diagonal,
    row_values,
    row_columns,
    weight_code,
    slot_count,
    slot_rows,
    local_inverse,
    coarse_modes,
    coarse_inverse,
):
    me = lax.axis_index("col")
    index = lax.broadcasted_iota(jnp.int32, (TEAM, SLOT), 1)
    coded = jnp.where(index < slot_count[0][:, None], slot_rows[0] + 1, 0)
    coded = lax.dynamic_slice_in_dim(coded, me, 1, axis=0)
    list_row = team_pass(coded, 1)
    fields = team_share(jnp.concatenate([start_field, adjoint_source], axis=0))
    list_rows = team_share(list_row)
    list_cols = [x.reshape(SLOT, 1) for x in list_rows]

    received = []
    for step in (1, 2, 3):
        at = jnp.where(me == 3, 128 * (step - 1), 384)
        piece = lax.dynamic_slice_in_dim(local_inverse, at, 128, axis=0)
        pairs = [(3 - step, 3), (3, step - 1)]
        received.append(lax.ppermute(piece, "col", pairs))

    lam, bvec, pick, slots, modes, inverse = call(
        setup_kernel,
        [
            ((4, ALLC, QUART), f32),
            ((ALLC, BLOCK), f32),
            ((4, QUART, SLOT), bf16),
            ((ALLC, SLOT), f32),
            ((4, 8, QUART), f32),
            ((8, SUBS * 8), f32),
        ],
        [((4, ALLC, QUART), f32)],
        400_000_000,
        2_000_000,
        *fields,
        list_row,
        coarse_modes,
        coarse_inverse,
    )
    slots = team_share(team_pass(slots, -1))
    (spread,) = call(lists_kernel, [((4, BLOCK, QUART), bf16)], [], 10_000_000, 2_000_000, *list_cols)
    s_high, s_low = call(
        operator_kernel,
        [((4, BLOCK, BLOCK), bf16), ((4, BLOCK, BLOCK), bf16)],
        [((32, BLOCK), f32), ((32, BLOCK), jnp.int32)],
        8_000_000_000,
        5_000_000,
        row_values,
        row_columns,
        row_diagonal.reshape(1, OWN),
        list_row,
        pick,
    )
    w_high, w_low = pl.pallas_call(
        inverse_kernel,
        grid=(4,),
        out_shape=[jax.ShapeDtypeStruct((4, BLOCK, BLOCK), bf16)] * 2,
        in_specs=[pl.BlockSpec((BLOCK, BLOCK), lambda i: (0, i))]
        + [pl.BlockSpec((128, BLOCK), lambda i: (0, i))] * 3
        + [pl.BlockSpec((1, BLOCK), lambda i: (0, i))],
        out_specs=[pl.BlockSpec((4, BLOCK, BLOCK), lambda i: (0, 0, 0))] * 2,
        compiler_params=pltpu.CompilerParams(vmem_limit_bytes=32 << 20),
        cost_estimate=pl.CostEstimate(flops=4_000_000_000, bytes_accessed=12_000_000, transcendentals=0),
    )(local_inverse, *received, weight_code.reshape(1, EXT))

    small = 600_000_000
    for iteration in range(ITERS):
        quarter, send = call(
            residual_kernel,
            [((ALLC, QUART), f32), ((ALLC, SLOT), f32)],
            [((4, ALLC, SLOT), f32)],
            small,
            5_000_000,
            lam,
            *slots,
            s_high,
            s_low,
            bvec,
        )
        blocks = team_share(jnp.concatenate([quarter, team_pass(send, -1)], axis=1))
        quarter, send, message = call(
            solve_kernel,
            [((ALLC, QUART), f32), ((ALLC, SLOT), f32), ((SUBS, 8, 128), f32)],
            [((4, ALLC, BLOCK), f32)],
            small,
            5_000_000,
            *blocks,
            w_high,
            w_low,
            modes,
        )
        coarse_rhs = lax.all_to_all(message, "sub", 0, 0).reshape(SUBS * 8, 128)
        blocks = team_share(jnp.concatenate([quarter, team_pass(send, 1)], axis=1))
        if iteration < ITERS - 1:
            lam, send = call(
                update_kernel,
                [((4, ALLC, QUART), f32), ((ALLC, SLOT), f32)],
                [((4, ALLC, BLOCK), f32)],
                small,
                3_000_000,
                *blocks,
                lam,
                spread,
                modes,
                inverse,
                coarse_rhs,
                pick,
            )
            slots = team_share(team_pass(send, -1))
        else:
            (values,) = call(
                final_kernel,
                [((COLS, OWN), f32)],
                [((4, ALLC, BLOCK), f32), ((4, ALLC, QUART), f32)],
                small,
                3_000_000,
                *blocks,
                lam,
                spread,
                modes,
                inverse,
                coarse_rhs,
            )
    return values


def solution(mesh):
    return jax.shard_map(
        local,
        mesh=mesh,
        in_specs=(
            P("col", "sub"),
            P("col", "sub"),
            P("sub"),
            P(None, "sub"),
            P(None, "sub"),
            P("sub"),
            P("sub", None),
            P("sub", None, None),
            P(("sub", "col"), None),
            P(None, "sub"),
            P("sub", None),
        ),
        out_specs=P("col", "sub"),
        check_vma=False,
    )
```

```python
import functools
import jax
import jax.numpy as jnp
from jax import lax
from jax.experimental import pallas as pl
from jax.experimental.pallas import tpu as pltpu
from jax.sharding import PartitionSpec as P

ITERS = 3
OWN = 1536
EXT = 2048
SLOT = 128
QUART = 384
BLOCK = 512
PART = 640
TERMS = 26
MODES = 4
SUBS = 64
TEAM = 4
COLS = 16
ALLC = 64

direction_steps = (-2, -1, 1, 2)
damping = 0.7
margin_holder = (1, 0, 2, 3)
highest = lax.Precision.HIGHEST
f32 = jnp.float32
bf16 = jnp.bfloat16
contract_last = (((1,), (1,)), ((), ()))
contract_first = (((0,), (0,)), ((), ()))


def source_of(member, step):
    return lax.rem(member - step + TEAM, TEAM)


def split(x):
    high = x.astype(bf16)
    low = (x - high.astype(f32)).astype(bf16)
    return high, low


def dot(a, b):
    return jnp.dot(a, b, preferred_element_type=f32)


def dot3(x, w_high, w_low):
    rows = x.shape[0]
    high, low = split(x)
    both = dot(jnp.concatenate([high, low], axis=0), w_high)
    return both[:rows] + both[rows:] + dot(high, w_low)


def dot2(x, ones):
    rows = x.shape[0]
    high, low = split(x)
    both = dot(jnp.concatenate([high, low], axis=0), ones)
    return both[:rows] + both[rows:]


def row_list(coded):
    return (coded + 0.5).astype(jnp.int32) - 1


def start_kernel(x0, x1, x2, x3, coded, modes, inverse, lam, pick, send):
    me = lax.axis_index("col")
    wanted = row_list(coded[...])
    for step, x in enumerate((x0, x1, x2, x3)):
        rows = pl.ds(pl.multiple_of(COLS * source_of(me, step), COLS), COLS)
        lam[rows, :] = x[...]
    for n in range(12):
        spot = lax.broadcasted_iota(jnp.int32, (128, SLOT), 0) + 128 * n
        pick[128 * n : 128 * n + 128, :] = (spot == wanted).astype(f32).astype(bf16)
    send[0:ALLC, :] = dot2(lam[...], pick[...])
    send[ALLC : ALLC + MODES, :] = jnp.dot(
        modes[...], pick[...].astype(f32), precision=highest, preferred_element_type=f32
    )
    send[ALLC + MODES : ALLC + 8, :] = jnp.zeros((MODES, SLOT), f32)
    send[ALLC + 8 : ALLC + 8 + MODES, :] = inverse[:, 0:128]
    send[ALLC + 8 + MODES : ALLC + 16, :] = inverse[:, 128:256]


def start_join_kernel(got, coded, out):
    out[0 : ALLC + 16, :] = got[...]
    out[ALLC + 16 :, :] = jnp.broadcast_to(coded[...], (8, SLOT))


def source_kernel(x0, x1, x2, x3, pick, modes, inverse, quarter, chosen, modes_out, inv_out, scr):
    me = lax.axis_index("col")
    for step, x in enumerate((x0, x1, x2, x3)):
        rows = pl.ds(pl.multiple_of(COLS * source_of(me, step), COLS), COLS)
        scr[rows, :] = x[...]
    for j in range(3):
        at = pl.ds(pl.multiple_of(QUART * me + 128 * j, 128), 128)
        quarter[:, 128 * j : 128 * j + 128] = scr[:, at]
    ones = pick[...].astype(f32)
    chosen[...] = jnp.dot(scr[...], ones, precision=highest, preferred_element_type=f32)
    modes_out[...] = jnp.zeros(modes_out.shape, f32)
    modes_out[0:MODES, :] = modes[...]
    width = SUBS * MODES
    at = lax.broadcasted_iota(jnp.int32, (width, SUBS * 8), 0)
    to = lax.broadcasted_iota(jnp.int32, (width, SUBS * 8), 1)
    spread = jnp.logical_and(at // MODES == to // 8, lax.rem(at, MODES) == lax.rem(to, 8)).astype(f32)
    inv_out[...] = jnp.zeros(inv_out.shape, f32)
    inv_out[0:MODES, :] = jnp.dot(inverse[...], spread, precision=highest, preferred_element_type=f32)


def lists_kernel(s0, s1, s2, s3, inverse, spread, margin_modes, near):
    me = lax.axis_index("col")
    width = SUBS * MODES
    at = lax.broadcasted_iota(jnp.int32, (width, width), 0)
    to = lax.broadcasted_iota(jnp.int32, (width, width), 1)
    turn = (at == lax.rem(to + MODES * lax.axis_index("sub"), width)).astype(f32)
    near[...] = jnp.zeros(near.shape, f32)

    def turned(left, right):
        return jnp.dot(
            jnp.concatenate([left, right], axis=1), turn, precision=highest, preferred_element_type=f32
        )

    near[4, 0:MODES, :] = turned(inverse[:, 0:128], inverse[:, 128:256])
    for step, s in enumerate((s0, s1, s2, s3)):
        source = source_of(me, step)
        margin_modes[source] = s[ALLC : ALLC + 8, :]
        near[source, 0:MODES, :] = turned(s[ALLC + 8 : ALLC + 12, :], s[ALLC + 12 : ALLC + 16, :])
        at = pl.multiple_of(SLOT * source, SLOT)
        coded = jnp.concatenate([s[ALLC + 16 :, :], jnp.zeros((120, SLOT), f32)], axis=0).T
        wanted = jnp.broadcast_to(row_list(coded[:, 0:1]), (SLOT, 128))
        for n in range(12):
            spot = lax.broadcasted_iota(jnp.int32, (SLOT, 128), 1) + 128 * n
            spread[pl.ds(at, SLOT), 128 * n : 128 * n + 128] = (spot == wanted).astype(f32).astype(bf16)


def dense(col, val, high, low, lanes):
    for b in range(4):
        for j in range(4):
            n = QUART * b + 128 * j if j < 3 else OWN + SLOT * b

            def body(q, carry, n=n, b=b, j=j):
                at = pl.multiple_of(q * 32, 32)
                spot = lax.broadcasted_iota(jnp.int32, (32, 128), 0) + (n + at)
                for lane in range(lanes):
                    to = slice(128 * lane, 128 * lane + 128)
                    total = jnp.zeros((32, 128), f32)
                    for term in range(TERMS + 1):
                        total = total + jnp.where(spot == col[term : term + 1, to], val[term : term + 1, to], 0.0)
                    first, second = split(total)
                    high[b, pl.ds(128 * j + at, 32), to] = first
                    low[b, pl.ds(128 * j + at, 32), to] = second
                return carry

            lax.fori_loop(0, 4, body, 0)


def quarter_kernel(values, columns, diagonal, high, low, val, col):
    me = lax.axis_index("col")
    for j in range(3):
        at = pl.ds(pl.multiple_of(QUART * me + 128 * j, 128), 128)
        to = slice(128 * j, 128 * j + 128)
        val[0:TERMS, to] = values[:, at]
        col[0:TERMS, to] = columns[:, at]
        val[TERMS : TERMS + 1, to] = diagonal[:, at]
        col[TERMS : TERMS + 1, to] = lax.broadcasted_iota(jnp.int32, (1, 128), 1) + (QUART * me + 128 * j)
    dense(col, val, high, low, 3)


def chosen_kernel(values, columns, diagonal, coded, pick, high, low, val, col):
    ones = pick[...].astype(f32)
    val[0:TERMS, :] = jnp.dot(values[...], ones, precision=highest, preferred_element_type=f32)
    found = jnp.dot(columns[...].astype(f32), ones, precision=highest, preferred_element_type=f32)
    col[0:TERMS, :] = (found + 0.5).astype(jnp.int32)
    diag = jnp.broadcast_to(diagonal[...], (8, OWN))
    val[TERMS : TERMS + 1, :] = jnp.dot(diag, ones, precision=highest, preferred_element_type=f32)[0:1]
    col[TERMS : TERMS + 1, :] = row_list(coded[...])
    dense(col, val, high, low, 1)


def inverse_kernel(owned, margin, code_owned, code_margin, high, low):
    for j in range(4):
        if j < 3:
            lanes = slice(128 * j, 128 * j + 128)
            tile, code = owned[:, lanes], code_owned[:, lanes]
        else:
            tile, code = margin[...], code_margin[...]
        first, second = split((tile * (1.0 / (1.0 + code.astype(f32)))).T)
        high[0, 128 * j : 128 * j + 128, :] = first
        low[0, 128 * j : 128 * j + 128, :] = second


def residual_of(lam, scr, q_high, q_low, c_high, c_low, source_q, source_c, quarter, slots):
    owned = jnp.zeros((ALLC, QUART), f32)
    chosen = jnp.zeros((ALLC, SLOT), f32)
    for b in range(4):
        x = jnp.concatenate([lam[:, QUART * b : QUART * b + QUART], scr[b]], axis=1)
        chosen = chosen + dot3(x, c_high[b], c_low[b])
        owned = owned + dot3(x, q_high[b], q_low[b])
    quarter[...] = source_q[...] - owned
    slots[...] = source_c[...] - chosen


def margin_kernel(first, third, code_owned, high, low):
    mine = lax.axis_index("col") == 0
    for b in range(4):
        for j in range(4):
            if j < 3:
                n = QUART * b + 128 * j
            else:
                n = OWN + SLOT * b
            lanes = slice(n, n + 128)
            tile = jnp.where(mine, first[:, lanes], third[:, lanes])
            code = code_owned[:, lanes]
            upper, lower = split((tile * (1.0 / (1.0 + code.astype(f32)))).T)
            high[b, 128 * j : 128 * j + 128, :] = upper
            low[b, 128 * j : 128 * j + 128, :] = lower


def first_residual_kernel(
    lam, s0, s1, s2, s3, q_high, q_low, c_high, c_low, source_q, source_c, quarter, slots, scr
):
    me = lax.axis_index("col")
    for step, s in enumerate((s0, s1, s2, s3)):
        scr[source_of(me, step)] = s[0:ALLC, :]
    residual_of(lam, scr, q_high, q_low, c_high, c_low, source_q, source_c, quarter, slots)


def residual_kernel(
    lam, s0, s1, s2, s3, q_high, q_low, c_high, c_low, source_q, source_c,
    modes, margin_modes, near, quarter, slots, out, scr, rhs,
):
    me = lax.axis_index("col")
    for step, s in enumerate((s0, s1, s2, s3)):
        rhs[source_of(me, step)] = s[ALLC:, :]
        scr[source_of(me, step)] = s[0:ALLC, :]
    coarse = jnp.dot(
        near[...].reshape(40, 256), rhs[...].reshape(256, 128), precision=highest, preferred_element_type=f32
    )
    coarse = jnp.concatenate([coarse, jnp.zeros((88, 128), f32)], axis=0).T[:ALLC]

    def lift(number, shape):
        return damping * jnp.dot(
            coarse[:, 8 * number : 8 * number + 8], shape, precision=highest, preferred_element_type=f32
        )

    for b in range(4):
        scr[b] = scr[b] + lift(b, margin_modes[b])
    for b in range(3):
        to = slice(BLOCK * b, BLOCK * b + BLOCK)
        out[:, to] = lam[:, to] + lift(4, modes[:, to])
    residual_of(out, scr, q_high, q_low, c_high, c_low, source_q, source_c, quarter, slots)


def residual_join_kernel(quarter, got, out):
    out[:, 0:QUART] = quarter[...]
    out[:, QUART:] = got[...]


def solve_kernel(x0, x1, x2, x3, high, low, m_high, m_low, modes, solved, send_a, send_b, message, scr):
    me = lax.axis_index("col")
    for step, x in enumerate((x0, x1, x2, x3)):
        scr[source_of(me, step)] = x[...]
    total = jnp.zeros((ALLC, BLOCK), f32)
    extra = jnp.zeros((ALLC, SLOT), f32)
    rhs = jnp.zeros((8, ALLC), f32)
    for b in range(4):
        x = scr[b]
        extra = extra + dot3(x, m_high[b], m_low[b])
        total = total + dot3(x, high[b], low[b])
        rhs = rhs + lax.dot_general(
            modes[:, QUART * b : QUART * b + QUART],
            x[:, :QUART],
            contract_last,
            precision=highest,
            preferred_element_type=f32,
        )
    rhs = jnp.concatenate([rhs, jnp.zeros((8, 128 - ALLC), f32)], axis=1)
    below = jnp.concatenate([rhs, jnp.zeros((ALLC - 8, 128), f32)], axis=0)
    solved[...] = total
    send_a[...] = jnp.where(me == 3, total[:, 3 * SLOT :], extra)
    send_b[...] = jnp.where(me == 3, total[:, SLOT : 2 * SLOT], below)
    message[...] = rhs


def coarse_part(inverse, coarse_rhs):
    coarse = jnp.dot(inverse[...], coarse_rhs[...], precision=highest, preferred_element_type=f32)
    return coarse.T


def field_part(lam, solved, back, spread, coarse, modes):
    lifted = jnp.dot(coarse, modes, precision=highest, preferred_element_type=f32)
    return lam + damping * (solved + dot2(back, spread) + lifted)


def solve_join_kernel(solved, got_a, got_b, message, odd, out):
    first = lax.axis_index("col") == 0
    out[0:ALLC, 0:BLOCK] = solved[...]
    out[0:ALLC, BLOCK:] = jnp.where(first, got_b[...], got_a[...])
    out[ALLC:, :] = jnp.zeros((8, PART), f32)
    out[ALLC : ALLC + MODES, 0:128] = jnp.where(first, message[0:MODES, :], got_b[0:MODES, :])
    out[ALLC + MODES : ALLC + 8, 0:128] = odd[0:MODES, :]


def final_join_kernel(solved, got_a, got_b, message, p0, p1, p2, p3, everyone, scr):
    me = lax.axis_index("col")
    scr[:, 0:BLOCK] = solved[...]
    scr[:, BLOCK:] = jnp.where(me == 0, got_b[...], got_a[...])
    for step, p in enumerate((p0, p1, p2, p3)):
        p[...] = scr[pl.ds(pl.multiple_of(COLS * lax.rem(me + step, TEAM), COLS), COLS), :]
    everyone[...] = jnp.broadcast_to(message[...][None], everyone.shape)


def update_kernel(x0, x1, x2, x3, lam, spread, pick, out, slots, entries, scr):
    me = lax.axis_index("col")
    for step, x in enumerate((x0, x1, x2, x3)):
        source = source_of(me, step)
        scr[source] = x[0:ALLC, :]
        entries[pl.ds(pl.multiple_of(8 * source, 8), 8), :] = x[ALLC:, 0:128]
    back = jnp.concatenate([scr[b, :, BLOCK:] for b in margin_holder], axis=1)
    send = jnp.zeros((ALLC, SLOT), f32)
    for b in range(3):
        to = slice(BLOCK * b, BLOCK * b + BLOCK)
        fresh = lam[:, to] + damping * (scr[b, :, :BLOCK] + dot2(back, spread[:, to]))
        out[:, to] = fresh
        send = send + dot2(fresh, pick[to, :])
    slots[...] = send


def update_join_kernel(got, entries, even, odd, out):
    first = lax.axis_index("col") == 0
    out[0:ALLC, :] = got[...]
    out[ALLC : ALLC + 32, :] = jnp.where(first, entries[...], even[...])
    out[ALLC + 32 :, :] = odd[...]


def final_kernel(x0, x1, x2, x3, lam, spread, modes, inverse, coarse_rhs, out, scr, across):
    me = lax.axis_index("col")
    for step, x in enumerate((x0, x1, x2, x3)):
        scr[source_of(me, step)] = x[...]
    rows = pl.ds(pl.multiple_of(COLS * me, COLS), COLS)
    back = jnp.concatenate([scr[b, :, BLOCK:] for b in margin_holder], axis=1)
    across[...] = coarse_part(inverse, coarse_rhs)
    coarse = across[rows, :]
    for b in range(3):
        to = slice(BLOCK * b, BLOCK * b + BLOCK)
        out[:, to] = field_part(lam[rows, to], scr[b, :, :BLOCK], back, spread[:, to], coarse, modes[:, to])


def call(kernel, outs, scratch, flops, nbytes, *args, after=(), limit=6 << 20):
    taken = len(args)

    def body(*refs):
        kernel(*refs[:taken], *refs[taken + len(after) :])

    return pl.pallas_call(
        body,
        out_shape=[jax.ShapeDtypeStruct(shape, dtype) for shape, dtype in outs],
        in_specs=[pl.BlockSpec(memory_space=pltpu.VMEM)] * taken
        + [pl.BlockSpec(memory_space=pl.ANY)] * len(after),
        out_specs=[pl.BlockSpec(memory_space=pltpu.VMEM)] * len(outs),
        scratch_shapes=[pltpu.VMEM(shape, dtype) for shape, dtype in scratch],
        compiler_params=pltpu.CompilerParams(vmem_limit_bytes=limit),
        cost_estimate=pl.CostEstimate(flops=flops, bytes_accessed=nbytes, transcendentals=0),
        name=kernel.__name__,
    )(*args, *after)


def team_pass(x, sign):
    pairs = []
    for s in range(SUBS):
        for d, step in enumerate(direction_steps):
            t = s + sign * step
            if 0 <= t < SUBS:
                pairs.append((s * TEAM + d, t * TEAM + d))
    return lax.ppermute(x, ("sub", "col"), pairs)


def margin_pass(send_a, send_b, with_coarse):
    first, second = [], []
    for s in range(SUBS):
        for d, source in ((0, 0), (2, 2), (3, 3), (1, 3)):
            t = s + direction_steps[d]
            if 0 <= t < SUBS:
                pair = (s * TEAM + source, t * TEAM + margin_holder[d])
                (second if d == 1 else first).append(pair)
        if with_coarse:
            for c in (1, 2, 3):
                second.append(((s + 2 * c) % SUBS * TEAM + c - 1, s * TEAM + c))
    axes = ("sub", "col")
    return lax.ppermute(send_a, axes, first), lax.ppermute(send_b, axes, second)


def coarse_pass(x, width, odd):
    pairs = [
        ((s + width * (2 * c + odd)) % SUBS * TEAM + c, s * TEAM + c)
        for s in range(SUBS)
        for c in range(TEAM)
        if 2 * c + odd > 0
    ]
    return lax.ppermute(x, ("sub", "col"), pairs)


def step_pass(x, step):
    return lax.ppermute(x, "col", [(i, (i + step) % TEAM) for i in range(TEAM)])


def team_share(x):
    return [x] + [step_pass(x, step) for step in (1, 2, 3)]


def local(
    adjoint_source,
    start_field,
    row_diagonal,
    row_values,
    row_columns,
    weight_code,
    slot_count,
    slot_rows,
    local_inverse,
    coarse_modes,
    coarse_inverse,
):
    me = lax.axis_index("col")
    index = lax.broadcasted_iota(jnp.int32, (TEAM, SLOT), 1)
    coded = jnp.where(index < slot_count[0][:, None], slot_rows[0] + 1, 0).astype(f32)
    coded = lax.dynamic_slice_in_dim(coded, me, 1, axis=0)
    coded = team_pass(coded, 1)
    fields = team_share(start_field)
    ring = [(3, 0)], [(3, 2)]
    first = lax.ppermute(local_inverse[0:SLOT], "col", ring[0])
    third = lax.ppermute(local_inverse[2 * SLOT : 3 * SLOT], "col", ring[1])
    diagonal = row_diagonal.reshape(1, OWN)
    code = weight_code.reshape(1, EXT)

    half = ((4, BLOCK, QUART), bf16)
    q_high, q_low = call(
        quarter_kernel,
        [half, half],
        [((32, QUART), f32), ((32, QUART), jnp.int32)],
        6_000_000_000,
        4_000_000,
        row_values,
        row_columns,
        diagonal,
    )
    lam, pick, slots = call(
        start_kernel,
        [((ALLC, OWN), f32), ((OWN, SLOT), bf16), ((ALLC + 16, SLOT), f32)],
        [],
        100_000_000,
        1_000_000,
        *fields,
        coded,
        coarse_modes,
        coarse_inverse,
        after=(q_low,),
    )
    adjoint_source, slots = lax.optimization_barrier((adjoint_source, slots))
    slots = team_pass(slots, -1)
    sources = team_share(adjoint_source)
    c_high, c_low = call(
        chosen_kernel,
        [((4, BLOCK, SLOT), bf16), ((4, BLOCK, SLOT), bf16)],
        [((32, SLOT), f32), ((32, SLOT), jnp.int32)],
        2_000_000_000,
        1_000_000,
        row_values,
        row_columns,
        diagonal,
        coded,
        pick,
    )
    (slots,) = call(start_join_kernel, [((ALLC + 24, SLOT), f32)], [], 0, 80_000, slots, coded, after=(c_low,))
    slots = team_share(slots)
    source_q, source_c, modes, inverse = call(
        source_kernel,
        [((ALLC, QUART), f32), ((ALLC, SLOT), f32), ((8, OWN), f32), ((8, SUBS * 8), f32)],
        [((ALLC, OWN), f32)],
        400_000_000,
        2_000_000,
        *sources,
        pick,
        coarse_modes,
        coarse_inverse,
    )
    w_high, w_low = pl.pallas_call(
        inverse_kernel,
        grid=(4,),
        out_shape=[jax.ShapeDtypeStruct((4, BLOCK, BLOCK), bf16)] * 2,
        in_specs=[
            pl.BlockSpec((BLOCK, QUART), lambda i: (0, i)),
            pl.BlockSpec((BLOCK, SLOT), lambda i: (0, 12 + i)),
            pl.BlockSpec((1, QUART), lambda i: (0, i)),
            pl.BlockSpec((1, SLOT), lambda i: (0, 12 + i)),
        ],
        out_specs=[pl.BlockSpec((1, BLOCK, BLOCK), lambda i: (i, 0, 0))] * 2,
        compiler_params=pltpu.CompilerParams(vmem_limit_bytes=12 << 20),
        cost_estimate=pl.CostEstimate(flops=4_000_000_000, bytes_accessed=8_000_000, transcendentals=0),
    )(local_inverse, local_inverse, code, code)
    m_high, m_low = call(
        margin_kernel,
        [((4, BLOCK, SLOT), bf16), ((4, BLOCK, SLOT), bf16)],
        [],
        1_000_000_000,
        3_000_000,
        first,
        third,
        code,
    )

    small = 600_000_000
    piece = ((ALLC, SLOT), f32)
    for iteration in range(ITERS):
        last = iteration == ITERS - 1
        operator = (q_high, q_low, c_high, c_low, source_q, source_c)
        if iteration == 0:
            quarter, send = call(
                first_residual_kernel,
                [((ALLC, QUART), f32), piece],
                [((4, ALLC, SLOT), f32)],
                small,
                5_000_000,
                lam,
                *slots,
                *operator,
            )
            spread, margin_modes, near = call(
                lists_kernel,
                [((BLOCK, OWN), bf16), ((4, 8, SLOT), f32), ((5, 8, 256), f32)],
                [],
                10_000_000,
                2_000_000,
                *slots,
                coarse_inverse,
            )
        else:
            quarter, send, lam = call(
                residual_kernel,
                [((ALLC, QUART), f32), piece, ((ALLC, OWN), f32)],
                [((4, ALLC, SLOT), f32), ((4, ALLC, 128), f32)],
                small,
                5_000_000,
                lam,
                *slots,
                *operator,
                modes,
                margin_modes,
                near,
            )
        (block,) = call(
            residual_join_kernel, [((ALLC, BLOCK), f32)], [], 0, 260_000, quarter, team_pass(send, -1)
        )
        solved, send_a, send_b, message = call(
            solve_kernel,
            [((ALLC, BLOCK), f32), piece, piece, ((8, 128), f32)],
            [((4, ALLC, BLOCK), f32)],
            small,
            5_000_000,
            *team_share(block),
            w_high,
            w_low,
            m_high,
            m_low,
            modes,
        )
        got = margin_pass(send_a, send_b, not last)
        if not last:
            odd = coarse_pass(message, 1, 1)
            (part,) = call(
                solve_join_kernel, [((ALLC + 8, PART), f32)], [], 0, 400_000, solved, *got, message, odd
            )
            lam, send, entries = call(
                update_kernel,
                [((ALLC, OWN), f32), piece, ((32, 128), f32)],
                [((4, ALLC, PART), f32)],
                small,
                3_000_000,
                *team_share(part),
                lam,
                spread,
                pick,
            )
            send = team_pass(send, -1)
            even, odd = coarse_pass(entries, 8, 0), coarse_pass(entries, 8, 1)
            (slots,) = call(
                update_join_kernel, [((2 * ALLC, SLOT), f32)], [], 0, 130_000, send, entries, even, odd
            )
            slots = team_share(slots)
        else:
            *parts, everyone = call(
                final_join_kernel,
                [((COLS, PART), f32)] * 4 + [((SUBS, 8, 128), f32)],
                [((ALLC, PART), f32)],
                0,
                400_000,
                solved,
                *got,
                message,
            )
            coarse_rhs = lax.all_to_all(everyone, "sub", 0, 0).reshape(SUBS * 8, 128)
            parts = [parts[0]] + [step_pass(parts[step], step) for step in (1, 2, 3)]
            (values,) = call(
                final_kernel,
                [((COLS, OWN), f32)],
                [((4, COLS, PART), f32), ((128, 8), f32)],
                small,
                3_000_000,
                *parts,
                lam,
                spread,
                modes,
                inverse,
                coarse_rhs,
            )
    return values


def solution(mesh):
    return jax.shard_map(
        local,
        mesh=mesh,
        in_specs=(
            P("col", "sub"),
            P("col", "sub"),
            P("sub"),
            P(None, "sub"),
            P(None, "sub"),
            P("sub"),
            P("sub", None),
            P("sub", None, None),
            P(("sub", "col"), None),
            P(None, "sub"),
            P("sub", None),
        ),
        out_specs=P("col", "sub"),
        check_vma=False,
    )
```

```python
import functools
import jax
import jax.numpy as jnp
from jax import lax
from jax.experimental import pallas as pl
from jax.experimental.pallas import tpu as pltpu
from jax.sharding import PartitionSpec as P

ITERS = 3
OWN = 1536
EXT = 2048
SLOT = 128
QUART = 384
BLOCK = 512
PART = 640
TERMS = 26
MODES = 4
SUBS = 64
TEAM = 4
COLS = 16
ALLC = 64

direction_steps = (-2, -1, 1, 2)
damping = 0.7
margin_holder = (1, 0, 2, 3)
highest = lax.Precision.HIGHEST
f32 = jnp.float32
bf16 = jnp.bfloat16
contract_last = (((1,), (1,)), ((), ()))
contract_first = (((0,), (0,)), ((), ()))


def source_of(member, step):
    return lax.rem(member - step + TEAM, TEAM)


def split(x):
    high = x.astype(bf16)
    low = (x - high.astype(f32)).astype(bf16)
    return high, low


def dot(a, b):
    return jnp.dot(a, b, preferred_element_type=f32)


def dot3(x, w_high, w_low):
    rows = x.shape[0]
    high, low = split(x)
    both = dot(jnp.concatenate([high, low], axis=0), w_high)
    return both[:rows] + both[rows:] + dot(high, w_low)


def dot2(x, ones):
    rows = x.shape[0]
    high, low = split(x)
    both = dot(jnp.concatenate([high, low], axis=0), ones)
    return both[:rows] + both[rows:]


def row_list(coded):
    return (coded + 0.5).astype(jnp.int32) - 1


def dot_exact(x, ones):
    rows = x.shape[0]
    high, rest = split(x)
    low = x - high.astype(f32)
    low = (low - rest.astype(f32)).astype(bf16)
    parts = dot(jnp.concatenate([high, rest, low], axis=0), ones)
    return (parts[2 * rows :] + parts[rows : 2 * rows]) + parts[:rows]


def list_kernel(count, rows, out):
    me = lax.axis_index("col")
    place = lax.broadcasted_iota(jnp.int32, (1, TEAM), 1)
    live = jnp.sum(jnp.where(place == me, count[...], 0), axis=1, keepdims=True)
    index = lax.broadcasted_iota(jnp.int32, (1, SLOT), 1)
    out[...] = jnp.where(index < live, rows[0, pl.ds(me, 1), :] + 1, 0).astype(f32)


def field_join_kernel(field, source, out):
    out[0:COLS, :] = field[...]
    out[COLS:, :] = source[...]


def start_kernel(x0, x1, x2, x3, coded, modes, inverse, lam, pick, send):
    me = lax.axis_index("col")
    wanted = row_list(coded[...])
    for step, x in enumerate((x0, x1, x2, x3)):
        rows = pl.ds(pl.multiple_of(COLS * source_of(me, step), COLS), COLS)
        lam[rows, :] = x[0:COLS, :]
    for n in range(12):
        spot = lax.broadcasted_iota(jnp.int32, (128, SLOT), 0) + 128 * n
        pick[128 * n : 128 * n + 128, :] = (spot == wanted).astype(f32).astype(bf16)
    send[0:ALLC, :] = dot2(lam[...], pick[...])
    send[ALLC : ALLC + MODES, :] = jnp.dot(
        modes[...], pick[...].astype(f32), precision=highest, preferred_element_type=f32
    )
    send[ALLC + MODES : ALLC + 8, :] = jnp.zeros((MODES, SLOT), f32)
    send[ALLC + 8 : ALLC + 8 + MODES, :] = inverse[:, 0:128]
    send[ALLC + 8 + MODES : ALLC + 16, :] = inverse[:, 128:256]


def start_join_kernel(got, coded, out):
    out[0 : ALLC + 16, :] = got[...]
    out[ALLC + 16 :, :] = jnp.broadcast_to(coded[...], (8, SLOT))


def source_kernel(x0, x1, x2, x3, pick, modes, inverse, quarter, chosen, modes_out, inv_out, scr):
    me = lax.axis_index("col")
    for step, x in enumerate((x0, x1, x2, x3)):
        rows = pl.ds(pl.multiple_of(COLS * source_of(me, step), COLS), COLS)
        scr[rows, :] = x[COLS:, :]
    for j in range(3):
        at = pl.ds(pl.multiple_of(QUART * me + 128 * j, 128), 128)
        quarter[:, 128 * j : 128 * j + 128] = scr[:, at]
    chosen[...] = dot_exact(scr[...], pick[...])
    modes_out[...] = jnp.zeros(modes_out.shape, f32)
    modes_out[0:MODES, :] = modes[...]
    width = SUBS * MODES
    at = lax.broadcasted_iota(jnp.int32, (width, SUBS * 8), 0)
    to = lax.broadcasted_iota(jnp.int32, (width, SUBS * 8), 1)
    spread = jnp.logical_and(at // MODES == to // 8, lax.rem(at, MODES) == lax.rem(to, 8)).astype(f32)
    inv_out[...] = jnp.zeros(inv_out.shape, f32)
    inv_out[0:MODES, :] = jnp.dot(inverse[...], spread, precision=highest, preferred_element_type=f32)


def lists_kernel(s0, s1, s2, s3, inverse, spread, margin_modes, near):
    me = lax.axis_index("col")
    width = SUBS * MODES
    at = lax.broadcasted_iota(jnp.int32, (width, width), 0)
    to = lax.broadcasted_iota(jnp.int32, (width, width), 1)
    turn = (at == lax.rem(to + MODES * lax.axis_index("sub"), width)).astype(f32)
    near[...] = jnp.zeros(near.shape, f32)

    def turned(left, right):
        return jnp.dot(
            jnp.concatenate([left, right], axis=1), turn, precision=highest, preferred_element_type=f32
        )

    near[4, 0:MODES, :] = turned(inverse[:, 0:128], inverse[:, 128:256])
    for step, s in enumerate((s0, s1, s2, s3)):
        source = source_of(me, step)
        margin_modes[source] = s[ALLC : ALLC + 8, :]
        near[source, 0:MODES, :] = turned(s[ALLC + 8 : ALLC + 12, :], s[ALLC + 12 : ALLC + 16, :])
        at = pl.multiple_of(SLOT * source, SLOT)
        coded = jnp.concatenate([s[ALLC + 16 :, :], jnp.zeros((120, SLOT), f32)], axis=0).T
        wanted = jnp.broadcast_to(row_list(coded[:, 0:1]), (SLOT, 128))
        for n in range(12):
            spot = lax.broadcasted_iota(jnp.int32, (SLOT, 128), 1) + 128 * n
            spread[pl.ds(at, SLOT), 128 * n : 128 * n + 128] = (spot == wanted).astype(f32).astype(bf16)


def dense(col, val, high, low, lanes):
    def body(group, carry):
        b, j = group // 16, lax.rem(group // 4, 4)
        first = jnp.where(j < 3, QUART * b + 128 * j, OWN + SLOT * b) + 32 * lax.rem(group, 4)
        rows = pl.ds(pl.multiple_of(group * 32, 32), 32)
        spot = lax.broadcasted_iota(jnp.int32, (32, 128), 0) + first
        for lane in range(lanes):
            to = slice(128 * lane, 128 * lane + 128)
            total = jnp.zeros((32, 128), f32)
            for term in range(TERMS + 1):
                total = total + jnp.where(spot == col[term : term + 1, to], val[term : term + 1, to], 0.0)
            high[rows, to], low[rows, to] = split(total)
        return carry

    lax.fori_loop(0, EXT // 32, body, 0)


def quarter_kernel(values, columns, diagonal, high, low, val, col):
    me = lax.axis_index("col")
    for j in range(3):
        at = pl.ds(pl.multiple_of(QUART * me + 128 * j, 128), 128)
        to = slice(128 * j, 128 * j + 128)
        val[0:TERMS, to] = values[:, at]
        col[0:TERMS, to] = columns[:, at]
        val[TERMS : TERMS + 1, to] = diagonal[:, at]
        col[TERMS : TERMS + 1, to] = lax.broadcasted_iota(jnp.int32, (1, 128), 1) + (QUART * me + 128 * j)
    dense(col, val, high, low, 3)


def chosen_kernel(values, columns, diagonal, coded, pick, high, low, val, col, rows):
    rows[...] = jnp.zeros(rows.shape, f32)
    rows[0:TERMS, :] = values[...]
    rows[32 : 32 + TERMS, :] = columns[...].astype(f32)
    rows[64:65, :] = diagonal[...]
    found = dot_exact(rows[...], pick[...])
    val[0:TERMS, :] = found[0:TERMS]
    col[0:TERMS, :] = (found[32 : 32 + TERMS] + 0.5).astype(jnp.int32)
    val[TERMS : TERMS + 1, :] = found[64:65]
    col[TERMS : TERMS + 1, :] = row_list(coded[...])
    dense(col, val, high, low, 1)


def inverse_kernel(owned, margin, code_owned, code_margin, high, low):
    for j in range(4):
        if j < 3:
            lanes = slice(128 * j, 128 * j + 128)
            tile, code = owned[:, lanes], code_owned[:, lanes]
        else:
            tile, code = margin[...], code_margin[...]
        first, second = split((tile * (1.0 / (1.0 + code.astype(f32)))).T)
        high[0, 128 * j : 128 * j + 128, :] = first
        low[0, 128 * j : 128 * j + 128, :] = second


def residual_of(lam, scr, q_high, q_low, c_high, c_low, source_q, source_c, quarter, slots):
    owned = jnp.zeros((ALLC, QUART), f32)
    chosen = jnp.zeros((ALLC, SLOT), f32)
    for b in range(4):
        x = jnp.concatenate([lam[:, QUART * b : QUART * b + QUART], scr[b]], axis=1)
        rows = slice(BLOCK * b, BLOCK * b + BLOCK)
        chosen = chosen + dot3(x, c_high[rows, :], c_low[rows, :])
        owned = owned + dot3(x, q_high[rows, :], q_low[rows, :])
    quarter[...] = source_q[...] - owned
    slots[...] = source_c[...] - chosen


def margin_kernel(first, third, code_owned, high, low):
    mine = lax.axis_index("col") == 0
    for b in range(4):
        for j in range(4):
            if j < 3:
                n = QUART * b + 128 * j
            else:
                n = OWN + SLOT * b
            lanes = slice(n, n + 128)
            tile = jnp.where(mine, first[:, lanes], third[:, lanes])
            code = code_owned[:, lanes]
            upper, lower = split((tile * (1.0 / (1.0 + code.astype(f32)))).T)
            high[b, 128 * j : 128 * j + 128, :] = upper
            low[b, 128 * j : 128 * j + 128, :] = lower


def first_residual_kernel(
    lam, s0, s1, s2, s3, q_high, q_low, c_high, c_low, source_q, source_c, quarter, slots, scr
):
    me = lax.axis_index("col")
    for step, s in enumerate((s0, s1, s2, s3)):
        scr[source_of(me, step)] = s[0:ALLC, :]
    residual_of(lam, scr, q_high, q_low, c_high, c_low, source_q, source_c, quarter, slots)


def residual_kernel(
    lam, s0, s1, s2, s3, q_high, q_low, c_high, c_low, source_q, source_c,
    modes, margin_modes, near, quarter, slots, out, scr, rhs,
):
    me = lax.axis_index("col")
    for step, s in enumerate((s0, s1, s2, s3)):
        rhs[source_of(me, step)] = s[ALLC:, :]
        scr[source_of(me, step)] = s[0:ALLC, :]
    coarse = jnp.dot(
        near[...].reshape(40, 256), rhs[...].reshape(256, 128), precision=highest, preferred_element_type=f32
    )
    coarse = jnp.concatenate([coarse, jnp.zeros((88, 128), f32)], axis=0).T[:ALLC]

    def lift(number, shape):
        return damping * jnp.dot(
            coarse[:, 8 * number : 8 * number + 8], shape, precision=highest, preferred_element_type=f32
        )

    for b in range(4):
        scr[b] = scr[b] + lift(b, margin_modes[b])
    for b in range(3):
        to = slice(BLOCK * b, BLOCK * b + BLOCK)
        out[:, to] = lam[:, to] + lift(4, modes[:, to])
    residual_of(out, scr, q_high, q_low, c_high, c_low, source_q, source_c, quarter, slots)


def residual_join_kernel(quarter, got, out):
    out[:, 0:QUART] = quarter[...]
    out[:, QUART:] = got[...]


def solve_kernel(x0, x1, x2, x3, high, low, m_high, m_low, modes, solved, send_a, send_b, message, scr):
    me = lax.axis_index("col")
    for step, x in enumerate((x0, x1, x2, x3)):
        scr[source_of(me, step)] = x[...]
    total = jnp.zeros((ALLC, BLOCK), f32)
    extra = jnp.zeros((ALLC, SLOT), f32)
    rhs = jnp.zeros((8, ALLC), f32)
    for b in range(4):
        x = scr[b]
        extra = extra + dot3(x, m_high[b], m_low[b])
        total = total + dot3(x, high[b], low[b])
        rhs = rhs + lax.dot_general(
            modes[:, QUART * b : QUART * b + QUART],
            x[:, :QUART],
            contract_last,
            precision=highest,
            preferred_element_type=f32,
        )
    rhs = jnp.concatenate([rhs, jnp.zeros((8, 128 - ALLC), f32)], axis=1)
    below = jnp.concatenate([rhs, jnp.zeros((ALLC - 8, 128), f32)], axis=0)
    solved[...] = total
    send_a[...] = jnp.where(me == 3, total[:, 3 * SLOT :], extra)
    send_b[...] = jnp.where(me == 3, total[:, SLOT : 2 * SLOT], below)
    message[...] = rhs


def coarse_part(inverse, coarse_rhs):
    coarse = jnp.dot(inverse[...], coarse_rhs[...], precision=highest, preferred_element_type=f32)
    return coarse.T


def field_part(lam, solved, back, spread, coarse, modes):
    lifted = jnp.dot(coarse, modes, precision=highest, preferred_element_type=f32)
    return lam + damping * (solved + dot2(back, spread) + lifted)


def entries_kernel(x0, x1, x2, x3, modes, everyone):
    me = lax.axis_index("col")
    rhs = jnp.zeros((8, ALLC), f32)
    for step, x in enumerate((x0, x1, x2, x3)):
        at = pl.ds(pl.multiple_of(QUART * source_of(me, step), 128), QUART)
        rhs = rhs + lax.dot_general(
            modes[:, at], x[:, 0:QUART], contract_last, precision=highest, preferred_element_type=f32
        )
    rhs = jnp.concatenate([rhs, jnp.zeros((8, 128 - ALLC), f32)], axis=1)
    everyone[...] = jnp.broadcast_to(rhs[None], everyone.shape)


def solve_join_kernel(solved, got_a, got_b, message, odd, out):
    first = lax.axis_index("col") == 0
    out[0:ALLC, 0:BLOCK] = solved[...]
    out[0:ALLC, BLOCK:] = jnp.where(first, got_b[...], got_a[...])
    out[ALLC:, :] = jnp.zeros((8, PART), f32)
    out[ALLC : ALLC + MODES, 0:128] = jnp.where(first, message[0:MODES, :], got_b[0:MODES, :])
    out[ALLC + MODES : ALLC + 8, 0:128] = odd[0:MODES, :]


def final_join_kernel(solved, got_a, got_b, p0, p1, p2, p3, scr):
    me = lax.axis_index("col")
    scr[:, 0:BLOCK] = solved[...]
    scr[:, BLOCK:] = jnp.where(me == 0, got_b[...], got_a[...])
    for step, p in enumerate((p0, p1, p2, p3)):
        p[...] = scr[pl.ds(pl.multiple_of(COLS * lax.rem(me + step, TEAM), COLS), COLS), :]


def update_kernel(x0, x1, x2, x3, lam, spread, pick, out, slots, entries, scr):
    me = lax.axis_index("col")
    for step, x in enumerate((x0, x1, x2, x3)):
        source = source_of(me, step)
        scr[source] = x[0:ALLC, :]
        entries[pl.ds(pl.multiple_of(8 * source, 8), 8), :] = x[ALLC:, 0:128]
    back = jnp.concatenate([scr[b, :, BLOCK:] for b in margin_holder], axis=1)
    send = jnp.zeros((ALLC, SLOT), f32)
    for b in range(3):
        to = slice(BLOCK * b, BLOCK * b + BLOCK)
        fresh = lam[:, to] + damping * (scr[b, :, :BLOCK] + dot2(back, spread[:, to]))
        out[:, to] = fresh
        send = send + dot2(fresh, pick[to, :])
    slots[...] = send


def update_join_kernel(got, entries, even, odd, out):
    first = lax.axis_index("col") == 0
    out[0:ALLC, :] = got[...]
    out[ALLC : ALLC + 32, :] = jnp.where(first, entries[...], even[...])
    out[ALLC + 32 :, :] = odd[...]


def final_kernel(x0, x1, x2, x3, lam, spread, modes, inverse, coarse_rhs, out, scr, across):
    me = lax.axis_index("col")
    for step, x in enumerate((x0, x1, x2, x3)):
        scr[source_of(me, step)] = x[...]
    rows = pl.ds(pl.multiple_of(COLS * me, COLS), COLS)
    back = jnp.concatenate([scr[b, :, BLOCK:] for b in margin_holder], axis=1)
    across[...] = coarse_part(inverse, coarse_rhs)
    coarse = across[rows, :]
    for b in range(3):
        to = slice(BLOCK * b, BLOCK * b + BLOCK)
        out[:, to] = field_part(lam[rows, to], scr[b, :, :BLOCK], back, spread[:, to], coarse, modes[:, to])


def call(kernel, outs, scratch, flops, nbytes, *args, after=(), limit=6 << 20):
    taken = len(args)

    def body(*refs):
        kernel(*refs[:taken], *refs[taken + len(after) :])

    return pl.pallas_call(
        body,
        out_shape=[jax.ShapeDtypeStruct(shape, dtype) for shape, dtype in outs],
        in_specs=[pl.BlockSpec(memory_space=pltpu.VMEM)] * taken
        + [pl.BlockSpec(memory_space=pl.ANY)] * len(after),
        out_specs=[pl.BlockSpec(memory_space=pltpu.VMEM)] * len(outs),
        scratch_shapes=[pltpu.VMEM(shape, dtype) for shape, dtype in scratch],
        compiler_params=pltpu.CompilerParams(vmem_limit_bytes=limit),
        cost_estimate=pl.CostEstimate(flops=flops, bytes_accessed=nbytes, transcendentals=0),
        name=kernel.__name__,
    )(*args, *after)


def team_pass(x, sign):
    pairs = []
    for s in range(SUBS):
        for d, step in enumerate(direction_steps):
            t = s + sign * step
            if 0 <= t < SUBS:
                pairs.append((s * TEAM + d, t * TEAM + d))
    return lax.ppermute(x, ("sub", "col"), pairs)


def margin_pass(send_a, send_b, with_coarse):
    first, second = [], []
    for s in range(SUBS):
        for d, source in ((0, 0), (2, 2), (3, 3), (1, 3)):
            t = s + direction_steps[d]
            if 0 <= t < SUBS:
                pair = (s * TEAM + source, t * TEAM + margin_holder[d])
                (second if d == 1 else first).append(pair)
        if with_coarse:
            for c in (1, 2, 3):
                second.append(((s + 2 * c) % SUBS * TEAM + c - 1, s * TEAM + c))
    axes = ("sub", "col")
    return lax.ppermute(send_a, axes, first), lax.ppermute(send_b, axes, second)


def coarse_pass(x, width, odd):
    pairs = [
        ((s + width * (2 * c + odd)) % SUBS * TEAM + c, s * TEAM + c)
        for s in range(SUBS)
        for c in range(TEAM)
        if 2 * c + odd > 0
    ]
    return lax.ppermute(x, ("sub", "col"), pairs)


def step_pass(x, step):
    return lax.ppermute(x, "col", [(i, (i + step) % TEAM) for i in range(TEAM)])


def team_share(x):
    return [x] + [step_pass(x, step) for step in (1, 2, 3)]


def local(
    adjoint_source,
    start_field,
    row_diagonal,
    row_values,
    row_columns,
    weight_code,
    slot_count,
    slot_rows,
    local_inverse,
    coarse_modes,
    coarse_inverse,
):
    (coded,) = call(list_kernel, [((1, SLOT), f32)], [], 0, 3_000, slot_count, slot_rows)
    coded = team_pass(coded, 1)
    (fields,) = call(field_join_kernel, [((2 * COLS, OWN), f32)], [], 0, 400_000, start_field, adjoint_source)
    fields = team_share(fields)
    ring = [(3, 0)], [(3, 2)]
    first = lax.ppermute(local_inverse[0:SLOT], "col", ring[0])
    third = lax.ppermute(local_inverse[2 * SLOT : 3 * SLOT], "col", ring[1])
    diagonal = row_diagonal.reshape(1, OWN)
    code = weight_code.reshape(1, EXT)

    half = ((EXT, QUART), bf16)
    q_high, q_low = call(
        quarter_kernel,
        [half, half],
        [((32, QUART), f32), ((32, QUART), jnp.int32)],
        6_000_000_000,
        4_000_000,
        row_values,
        row_columns,
        diagonal,
    )
    lam, pick, slots = call(
        start_kernel,
        [((ALLC, OWN), f32), ((OWN, SLOT), bf16), ((ALLC + 16, SLOT), f32)],
        [],
        100_000_000,
        1_000_000,
        *fields,
        coded,
        coarse_modes,
        coarse_inverse,
        after=(q_low,),
    )
    slots = team_pass(slots, -1)
    c_high, c_low = call(
        chosen_kernel,
        [((EXT, SLOT), bf16), ((EXT, SLOT), bf16)],
        [((32, SLOT), f32), ((32, SLOT), jnp.int32), ((80, OWN), f32)],
        2_000_000_000,
        1_000_000,
        row_values,
        row_columns,
        diagonal,
        coded,
        pick,
    )
    (slots,) = call(start_join_kernel, [((ALLC + 24, SLOT), f32)], [], 0, 80_000, slots, coded, after=(c_low,))
    slots = team_share(slots)
    source_q, source_c, modes, inverse = call(
        source_kernel,
        [((ALLC, QUART), f32), ((ALLC, SLOT), f32), ((8, OWN), f32), ((8, SUBS * 8), f32)],
        [((ALLC, OWN), f32)],
        400_000_000,
        2_000_000,
        *fields,
        pick,
        coarse_modes,
        coarse_inverse,
    )
    w_high, w_low = pl.pallas_call(
        inverse_kernel,
        grid=(4,),
        out_shape=[jax.ShapeDtypeStruct((4, BLOCK, BLOCK), bf16)] * 2,
        in_specs=[
            pl.BlockSpec((BLOCK, QUART), lambda i: (0, i)),
            pl.BlockSpec((BLOCK, SLOT), lambda i: (0, 12 + i)),
            pl.BlockSpec((1, QUART), lambda i: (0, i)),
            pl.BlockSpec((1, SLOT), lambda i: (0, 12 + i)),
        ],
        out_specs=[pl.BlockSpec((1, BLOCK, BLOCK), lambda i: (i, 0, 0))] * 2,
        compiler_params=pltpu.CompilerParams(vmem_limit_bytes=12 << 20),
        cost_estimate=pl.CostEstimate(flops=4_000_000_000, bytes_accessed=8_000_000, transcendentals=0),
    )(local_inverse, local_inverse, code, code)
    m_high, m_low = call(
        margin_kernel,
        [((4, BLOCK, SLOT), bf16), ((4, BLOCK, SLOT), bf16)],
        [],
        1_000_000_000,
        3_000_000,
        first,
        third,
        code,
    )

    small = 600_000_000
    piece = ((ALLC, SLOT), f32)
    for iteration in range(ITERS):
        last = iteration == ITERS - 1
        operator = (q_high, q_low, c_high, c_low, source_q, source_c)
        if iteration == 0:
            quarter, send = call(
                first_residual_kernel,
                [((ALLC, QUART), f32), piece],
                [((4, ALLC, SLOT), f32)],
                small,
                5_000_000,
                lam,
                *slots,
                *operator,
            )
            spread, margin_modes, near = call(
                lists_kernel,
                [((BLOCK, OWN), bf16), ((4, 8, SLOT), f32), ((5, 8, 256), f32)],
                [],
                10_000_000,
                2_000_000,
                *slots,
                coarse_inverse,
            )
        else:
            quarter, send, lam = call(
                residual_kernel,
                [((ALLC, QUART), f32), piece, ((ALLC, OWN), f32)],
                [((4, ALLC, SLOT), f32), ((4, ALLC, 128), f32)],
                small,
                5_000_000,
                lam,
                *slots,
                *operator,
                modes,
                margin_modes,
                near,
            )
        (block,) = call(
            residual_join_kernel, [((ALLC, BLOCK), f32)], [], 0, 260_000, quarter, team_pass(send, -1)
        )
        blocks = team_share(block)
        solved, send_a, send_b, message = call(
            solve_kernel,
            [((ALLC, BLOCK), f32), piece, piece, ((8, 128), f32)],
            [((4, ALLC, BLOCK), f32)],
            small,
            5_000_000,
            *blocks,
            w_high,
            w_low,
            m_high,
            m_low,
            modes,
        )
        got = margin_pass(send_a, send_b, not last)
        if not last:
            odd = coarse_pass(message, 1, 1)
            (part,) = call(
                solve_join_kernel, [((ALLC + 8, PART), f32)], [], 0, 400_000, solved, *got, message, odd
            )
            lam, send, entries = call(
                update_kernel,
                [((ALLC, OWN), f32), piece, ((32, 128), f32)],
                [((4, ALLC, PART), f32)],
                small,
                3_000_000,
                *team_share(part),
                lam,
                spread,
                pick,
            )
            send = team_pass(send, -1)
            even, odd = coarse_pass(entries, 8, 0), coarse_pass(entries, 8, 1)
            (slots,) = call(
                update_join_kernel, [((2 * ALLC, SLOT), f32)], [], 0, 130_000, send, entries, even, odd
            )
            slots = team_share(slots)
        else:
            (everyone,) = call(
                entries_kernel,
                [((SUBS, 8, 128), f32)],
                [],
                10_000_000,
                700_000,
                *blocks,
                modes,
                after=(got[0],),
            )
            coarse_rhs = lax.all_to_all(everyone, "sub", 0, 0).reshape(SUBS * 8, 128)
            parts = call(
                final_join_kernel,
                [((COLS, PART), f32)] * 4,
                [((ALLC, PART), f32)],
                0,
                400_000,
                solved,
                *got,
            )
            parts = [parts[0]] + [step_pass(parts[step], step) for step in (1, 2, 3)]
            (values,) = call(
                final_kernel,
                [((COLS, OWN), f32)],
                [((4, COLS, PART), f32), ((128, 8), f32)],
                small,
                3_000_000,
                *parts,
                lam,
                spread,
                modes,
                inverse,
                coarse_rhs,
            )
    return values


def solution(mesh):
    return jax.shard_map(
        local,
        mesh=mesh,
        in_specs=(
            P("col", "sub"),
            P("col", "sub"),
            P("sub"),
            P(None, "sub"),
            P(None, "sub"),
            P("sub"),
            P("sub", None),
            P("sub", None, None),
            P(("sub", "col"), None),
            P(None, "sub"),
            P("sub", None),
        ),
        out_specs=P("col", "sub"),
        check_vma=False,
    )
```

```python
import functools
import jax
import jax.numpy as jnp
from jax import lax
from jax.experimental import pallas as pl
from jax.experimental.pallas import tpu as pltpu
from jax.sharding import PartitionSpec as P

ITERS = 3
OWN = 1536
EXT = 2048
SLOT = 128
QUART = 384
BLOCK = 512
PART = 640
TERMS = 26
MODES = 4
SUBS = 64
TEAM = 4
COLS = 16
ALLC = 64

direction_steps = (-2, -1, 1, 2)
damping = 0.7
margin_holder = (1, 0, 2, 3)
highest = lax.Precision.HIGHEST
f32 = jnp.float32
bf16 = jnp.bfloat16
contract_last = (((1,), (1,)), ((), ()))
contract_first = (((0,), (0,)), ((), ()))


def source_of(member, step):
    return lax.rem(member - step + TEAM, TEAM)


def split(x):
    high = x.astype(bf16)
    low = (x - high.astype(f32)).astype(bf16)
    return high, low


def dot(a, b):
    return jnp.dot(a, b, preferred_element_type=f32)


def dot3(x, w_high, w_low):
    rows = x.shape[0]
    high, low = split(x)
    both = dot(jnp.concatenate([high, low], axis=0), w_high)
    return both[:rows] + both[rows:] + dot(high, w_low)


def dot2(x, ones):
    rows = x.shape[0]
    high, low = split(x)
    both = dot(jnp.concatenate([high, low], axis=0), ones)
    return both[:rows] + both[rows:]


def row_list(coded):
    return (coded + 0.5).astype(jnp.int32) - 1


def dot_exact(x, ones):
    rows = x.shape[0]
    high, rest = split(x)
    low = x - high.astype(f32)
    low = (low - rest.astype(f32)).astype(bf16)
    parts = dot(jnp.concatenate([high, rest, low], axis=0), ones)
    return (parts[2 * rows :] + parts[rows : 2 * rows]) + parts[:rows]


def list_kernel(count, rows, out):
    me = lax.axis_index("col")
    place = lax.broadcasted_iota(jnp.int32, (1, TEAM), 1)
    live = jnp.sum(jnp.where(place == me, count[...], 0), axis=1, keepdims=True)
    index = lax.broadcasted_iota(jnp.int32, (1, SLOT), 1)
    out[...] = jnp.where(index < live, rows[0, pl.ds(me, 1), :] + 1, 0).astype(f32)


def field_join_kernel(field, source, out):
    out[0:COLS, :] = field[...]
    out[COLS:, :] = source[...]


def start_kernel(x0, x1, x2, x3, coded, modes, inverse, lam, pick, send):
    me = lax.axis_index("col")
    wanted = row_list(coded[...])
    for step, x in enumerate((x0, x1, x2, x3)):
        rows = pl.ds(pl.multiple_of(COLS * source_of(me, step), COLS), COLS)
        lam[rows, :] = x[0:COLS, :]
    for n in range(12):
        spot = lax.broadcasted_iota(jnp.int32, (128, SLOT), 0) + 128 * n
        pick[128 * n : 128 * n + 128, :] = (spot == wanted).astype(f32).astype(bf16)
    send[0:ALLC, :] = dot2(lam[...], pick[...])
    send[ALLC : ALLC + MODES, :] = jnp.dot(
        modes[...], pick[...].astype(f32), precision=highest, preferred_element_type=f32
    )
    send[ALLC + MODES : ALLC + 8, :] = jnp.zeros((MODES, SLOT), f32)
    send[ALLC + 8 : ALLC + 8 + MODES, :] = inverse[:, 0:128]
    send[ALLC + 8 + MODES : ALLC + 16, :] = inverse[:, 128:256]


def start_join_kernel(got, coded, out):
    out[0 : ALLC + 16, :] = got[...]
    out[ALLC + 16 :, :] = jnp.broadcast_to(coded[...], (8, SLOT))


def source_kernel(x0, x1, x2, x3, pick, modes, inverse, quarter, chosen, modes_out, inv_out, scr):
    me = lax.axis_index("col")
    for step, x in enumerate((x0, x1, x2, x3)):
        rows = pl.ds(pl.multiple_of(COLS * source_of(me, step), COLS), COLS)
        scr[rows, :] = x[COLS:, :]
    for j in range(3):
        at = pl.ds(pl.multiple_of(QUART * me + 128 * j, 128), 128)
        quarter[:, 128 * j : 128 * j + 128] = scr[:, at]
    chosen[...] = dot_exact(scr[...], pick[...])
    modes_out[...] = jnp.zeros(modes_out.shape, f32)
    modes_out[0:MODES, :] = modes[...]
    width = SUBS * MODES
    at = lax.broadcasted_iota(jnp.int32, (width, SUBS * 8), 0)
    to = lax.broadcasted_iota(jnp.int32, (width, SUBS * 8), 1)
    spread = jnp.logical_and(at // MODES == to // 8, lax.rem(at, MODES) == lax.rem(to, 8)).astype(f32)
    inv_out[...] = jnp.zeros(inv_out.shape, f32)
    inv_out[0:MODES, :] = jnp.dot(inverse[...], spread, precision=highest, preferred_element_type=f32)


def lists_kernel(s0, s1, s2, s3, inverse, spread, margin_modes, near):
    me = lax.axis_index("col")
    width = SUBS * MODES
    at = lax.broadcasted_iota(jnp.int32, (width, width), 0)
    to = lax.broadcasted_iota(jnp.int32, (width, width), 1)
    other = lax.bitwise_xor(to // MODES, lax.axis_index("sub").astype(jnp.int32))
    turn = (at == MODES * other + lax.rem(to, MODES)).astype(f32)
    near[...] = jnp.zeros(near.shape, f32)

    def turned(left, right):
        return jnp.dot(
            jnp.concatenate([left, right], axis=1), turn, precision=highest, preferred_element_type=f32
        )

    near[4, 0:MODES, :] = turned(inverse[:, 0:128], inverse[:, 128:256])
    for step, s in enumerate((s0, s1, s2, s3)):
        source = source_of(me, step)
        margin_modes[source] = s[ALLC : ALLC + 8, :]
        near[source, 0:MODES, :] = turned(s[ALLC + 8 : ALLC + 12, :], s[ALLC + 12 : ALLC + 16, :])
        at = pl.multiple_of(SLOT * source, SLOT)
        coded = jnp.concatenate([s[ALLC + 16 :, :], jnp.zeros((120, SLOT), f32)], axis=0).T
        wanted = jnp.broadcast_to(row_list(coded[:, 0:1]), (SLOT, 128))
        for n in range(12):
            spot = lax.broadcasted_iota(jnp.int32, (SLOT, 128), 1) + 128 * n
            spread[pl.ds(at, SLOT), 128 * n : 128 * n + 128] = (spot == wanted).astype(f32).astype(bf16)


def dense(col, val, high, low, lanes):
    def body(group, carry):
        b, j = group // 16, lax.rem(group // 4, 4)
        first = jnp.where(j < 3, QUART * b + 128 * j, OWN + SLOT * b) + 32 * lax.rem(group, 4)
        rows = pl.ds(pl.multiple_of(group * 32, 32), 32)
        spot = lax.broadcasted_iota(jnp.int32, (32, 128), 0) + first
        for lane in range(lanes):
            to = slice(128 * lane, 128 * lane + 128)
            total = jnp.zeros((32, 128), f32)
            for term in range(TERMS + 1):
                total = total + jnp.where(spot == col[term : term + 1, to], val[term : term + 1, to], 0.0)
            high[rows, to], low[rows, to] = split(total)
        return carry

    lax.fori_loop(0, EXT // 32, body, 0)


def quarter_kernel(values, columns, diagonal, high, low, val, col):
    me = lax.axis_index("col")
    for j in range(3):
        at = pl.ds(pl.multiple_of(QUART * me + 128 * j, 128), 128)
        to = slice(128 * j, 128 * j + 128)
        val[0:TERMS, to] = values[:, at]
        col[0:TERMS, to] = columns[:, at]
        val[TERMS : TERMS + 1, to] = diagonal[:, at]
        col[TERMS : TERMS + 1, to] = lax.broadcasted_iota(jnp.int32, (1, 128), 1) + (QUART * me + 128 * j)
    dense(col, val, high, low, 3)


def chosen_kernel(values, columns, diagonal, coded, pick, high, low, val, col, rows):
    rows[...] = jnp.zeros(rows.shape, f32)
    rows[0:TERMS, :] = values[...]
    rows[32 : 32 + TERMS, :] = columns[...].astype(f32)
    rows[64:65, :] = diagonal[...]
    found = dot_exact(rows[...], pick[...])
    val[0:TERMS, :] = found[0:TERMS]
    col[0:TERMS, :] = (found[32 : 32 + TERMS] + 0.5).astype(jnp.int32)
    val[TERMS : TERMS + 1, :] = found[64:65]
    col[TERMS : TERMS + 1, :] = row_list(coded[...])
    dense(col, val, high, low, 1)


def inverse_kernel(owned, margin, code_owned, code_margin, high, low):
    for j in range(4):
        if j < 3:
            lanes = slice(128 * j, 128 * j + 128)
            tile, code = owned[:, lanes], code_owned[:, lanes]
        else:
            tile, code = margin[...], code_margin[...]
        first, second = split((tile * (1.0 / (1.0 + code.astype(f32)))).T)
        high[0, 128 * j : 128 * j + 128, :] = first
        low[0, 128 * j : 128 * j + 128, :] = second


def residual_of(lam, scr, q_high, q_low, c_high, c_low, source_q, source_c, quarter, slots):
    owned = jnp.zeros((ALLC, QUART), f32)
    chosen = jnp.zeros((ALLC, SLOT), f32)
    for b in range(4):
        x = jnp.concatenate([lam[:, QUART * b : QUART * b + QUART], scr[b]], axis=1)
        rows = slice(BLOCK * b, BLOCK * b + BLOCK)
        chosen = chosen + dot3(x, c_high[rows, :], c_low[rows, :])
        owned = owned + dot3(x, q_high[rows, :], q_low[rows, :])
    quarter[...] = source_q[...] - owned
    slots[...] = source_c[...] - chosen


def margin_kernel(first, third, code_owned, high, low):
    mine = lax.axis_index("col") == 0
    for b in range(4):
        for j in range(4):
            if j < 3:
                n = QUART * b + 128 * j
            else:
                n = OWN + SLOT * b
            lanes = slice(n, n + 128)
            tile = jnp.where(mine, first[:, lanes], third[:, lanes])
            code = code_owned[:, lanes]
            upper, lower = split((tile * (1.0 / (1.0 + code.astype(f32)))).T)
            high[b, 128 * j : 128 * j + 128, :] = upper
            low[b, 128 * j : 128 * j + 128, :] = lower


def first_residual_kernel(
    lam, s0, s1, s2, s3, q_high, q_low, c_high, c_low, source_q, source_c, quarter, slots, scr
):
    me = lax.axis_index("col")
    for step, s in enumerate((s0, s1, s2, s3)):
        scr[source_of(me, step)] = s[0:ALLC, :]
    residual_of(lam, scr, q_high, q_low, c_high, c_low, source_q, source_c, quarter, slots)


def residual_kernel(
    lam, s0, s1, s2, s3, q_high, q_low, c_high, c_low, source_q, source_c,
    modes, margin_modes, near, quarter, slots, out, scr, rhs,
):
    me = lax.axis_index("col")
    for step, s in enumerate((s0, s1, s2, s3)):
        rhs[source_of(me, step)] = s[ALLC:, :]
        scr[source_of(me, step)] = s[0:ALLC, :]
    coarse = jnp.dot(
        near[...].reshape(40, 256), rhs[...].reshape(256, 128), precision=highest, preferred_element_type=f32
    )
    coarse = jnp.concatenate([coarse, jnp.zeros((88, 128), f32)], axis=0).T[:ALLC]

    def lift(number, shape):
        return damping * jnp.dot(
            coarse[:, 8 * number : 8 * number + 8], shape, precision=highest, preferred_element_type=f32
        )

    for b in range(4):
        scr[b] = scr[b] + lift(b, margin_modes[b])
    for b in range(3):
        to = slice(BLOCK * b, BLOCK * b + BLOCK)
        out[:, to] = lam[:, to] + lift(4, modes[:, to])
    residual_of(out, scr, q_high, q_low, c_high, c_low, source_q, source_c, quarter, slots)


def residual_join_kernel(quarter, got, out):
    out[:, 0:QUART] = quarter[...]
    out[:, QUART:] = got[...]


def solve_kernel(x0, x1, x2, x3, high, low, m_high, m_low, modes, solved, send_a, send_b, message, scr):
    me = lax.axis_index("col")
    for step, x in enumerate((x0, x1, x2, x3)):
        scr[source_of(me, step)] = x[...]
    total = jnp.zeros((ALLC, BLOCK), f32)
    extra = jnp.zeros((ALLC, SLOT), f32)
    rhs = jnp.zeros((8, ALLC), f32)
    for b in range(4):
        x = scr[b]
        extra = extra + dot3(x, m_high[b], m_low[b])
        total = total + dot3(x, high[b], low[b])
        rhs = rhs + lax.dot_general(
            modes[:, QUART * b : QUART * b + QUART],
            x[:, :QUART],
            contract_last,
            precision=highest,
            preferred_element_type=f32,
        )
    rhs = jnp.concatenate([rhs, jnp.zeros((8, 128 - ALLC), f32)], axis=1)
    below = jnp.concatenate([rhs, jnp.zeros((ALLC - 8, 128), f32)], axis=0)
    solved[...] = total
    send_a[...] = jnp.where(me == 3, total[:, 3 * SLOT :], extra)
    send_b[...] = jnp.where(me == 3, total[:, SLOT : 2 * SLOT], below)
    message[...] = rhs


def coarse_part(inverse, coarse_rhs):
    coarse = jnp.dot(inverse[...], coarse_rhs[...], precision=highest, preferred_element_type=f32)
    return coarse.T


def field_part(lam, solved, back, spread, coarse, modes):
    lifted = jnp.dot(coarse, modes, precision=highest, preferred_element_type=f32)
    return lam + damping * (solved + dot2(back, spread) + lifted)


def entries_kernel(x0, x1, x2, x3, modes, everyone):
    me = lax.axis_index("col")
    rhs = jnp.zeros((8, ALLC), f32)
    for step, x in enumerate((x0, x1, x2, x3)):
        at = pl.ds(pl.multiple_of(QUART * source_of(me, step), 128), QUART)
        rhs = rhs + lax.dot_general(
            modes[:, at], x[:, 0:QUART], contract_last, precision=highest, preferred_element_type=f32
        )
    rhs = jnp.concatenate([rhs, jnp.zeros((8, 128 - ALLC), f32)], axis=1)
    everyone[...] = jnp.broadcast_to(rhs[None], everyone.shape)


def solve_join_kernel(solved, got_a, got_b, message, odd, out):
    first = lax.axis_index("col") == 0
    out[0:ALLC, 0:BLOCK] = solved[...]
    out[0:ALLC, BLOCK:] = jnp.where(first, got_b[...], got_a[...])
    out[ALLC:, :] = jnp.zeros((8, PART), f32)
    out[ALLC : ALLC + MODES, 0:128] = jnp.where(first, message[0:MODES, :], got_b[0:MODES, :])
    out[ALLC + MODES : ALLC + 8, 0:128] = odd[0:MODES, :]


def final_join_kernel(solved, got_a, got_b, p0, p1, p2, p3, scr):
    me = lax.axis_index("col")
    scr[:, 0:BLOCK] = solved[...]
    scr[:, BLOCK:] = jnp.where(me == 0, got_b[...], got_a[...])
    for step, p in enumerate((p0, p1, p2, p3)):
        p[...] = scr[pl.ds(pl.multiple_of(COLS * lax.rem(me + step, TEAM), COLS), COLS), :]


def update_kernel(x0, x1, x2, x3, lam, spread, pick, out, slots, entries, scr):
    me = lax.axis_index("col")
    for step, x in enumerate((x0, x1, x2, x3)):
        source = source_of(me, step)
        scr[source] = x[0:ALLC, :]
        entries[pl.ds(pl.multiple_of(8 * source, 8), 8), :] = x[ALLC:, 0:128]
    back = jnp.concatenate([scr[b, :, BLOCK:] for b in margin_holder], axis=1)
    send = jnp.zeros((ALLC, SLOT), f32)
    for b in range(3):
        to = slice(BLOCK * b, BLOCK * b + BLOCK)
        fresh = lam[:, to] + damping * (scr[b, :, :BLOCK] + dot2(back, spread[:, to]))
        out[:, to] = fresh
        send = send + dot2(fresh, pick[to, :])
    slots[...] = send


def update_join_kernel(got, entries, even, odd, out):
    first = lax.axis_index("col") == 0
    out[0:ALLC, :] = got[...]
    out[ALLC : ALLC + 32, :] = jnp.where(first, entries[...], even[...])
    out[ALLC + 32 :, :] = odd[...]


def final_kernel(x0, x1, x2, x3, lam, spread, modes, inverse, coarse_rhs, out, scr, across):
    me = lax.axis_index("col")
    for step, x in enumerate((x0, x1, x2, x3)):
        scr[source_of(me, step)] = x[...]
    rows = pl.ds(pl.multiple_of(COLS * me, COLS), COLS)
    back = jnp.concatenate([scr[b, :, BLOCK:] for b in margin_holder], axis=1)
    across[...] = coarse_part(inverse, coarse_rhs)
    coarse = across[rows, :]
    for b in range(3):
        to = slice(BLOCK * b, BLOCK * b + BLOCK)
        out[:, to] = field_part(lam[rows, to], scr[b, :, :BLOCK], back, spread[:, to], coarse, modes[:, to])


def call(kernel, outs, scratch, flops, nbytes, *args, after=(), limit=6 << 20):
    taken = len(args)

    def body(*refs):
        kernel(*refs[:taken], *refs[taken + len(after) :])

    return pl.pallas_call(
        body,
        out_shape=[jax.ShapeDtypeStruct(shape, dtype) for shape, dtype in outs],
        in_specs=[pl.BlockSpec(memory_space=pltpu.VMEM)] * taken
        + [pl.BlockSpec(memory_space=pl.ANY)] * len(after),
        out_specs=[pl.BlockSpec(memory_space=pltpu.VMEM)] * len(outs),
        scratch_shapes=[pltpu.VMEM(shape, dtype) for shape, dtype in scratch],
        compiler_params=pltpu.CompilerParams(vmem_limit_bytes=limit),
        cost_estimate=pl.CostEstimate(flops=flops, bytes_accessed=nbytes, transcendentals=0),
        name=kernel.__name__,
    )(*args, *after)


def team_pass(x, sign):
    pairs = []
    for s in range(SUBS):
        for d, step in enumerate(direction_steps):
            t = s + sign * step
            if 0 <= t < SUBS:
                pairs.append((s * TEAM + d, t * TEAM + d))
    return lax.ppermute(x, ("sub", "col"), pairs)


def margin_pass(send_a, send_b, with_coarse):
    first, second = [], []
    for s in range(SUBS):
        for d, source in ((0, 0), (2, 2), (3, 3), (1, 3)):
            t = s + direction_steps[d]
            if 0 <= t < SUBS:
                pair = (s * TEAM + source, t * TEAM + margin_holder[d])
                (second if d == 1 else first).append(pair)
        if with_coarse:
            for c in (1, 2, 3):
                second.append(((s ^ (2 * c)) * TEAM + c - 1, s * TEAM + c))
    axes = ("sub", "col")
    return lax.ppermute(send_a, axes, first), lax.ppermute(send_b, axes, second)


def coarse_pass(x, width, odd):
    pairs = [
        ((s ^ (width * (2 * c + odd))) * TEAM + c, s * TEAM + c)
        for s in range(SUBS)
        for c in range(TEAM)
        if 2 * c + odd > 0
    ]
    return lax.ppermute(x, ("sub", "col"), pairs)


def step_pass(x, step):
    return lax.ppermute(x, "col", [(i, (i + step) % TEAM) for i in range(TEAM)])


def team_share(x):
    return [x] + [step_pass(x, step) for step in (1, 2, 3)]


def local(
    adjoint_source,
    start_field,
    row_diagonal,
    row_values,
    row_columns,
    weight_code,
    slot_count,
    slot_rows,
    local_inverse,
    coarse_modes,
    coarse_inverse,
):
    (coded,) = call(list_kernel, [((1, SLOT), f32)], [], 0, 3_000, slot_count, slot_rows)
    coded = team_pass(coded, 1)
    (fields,) = call(field_join_kernel, [((2 * COLS, OWN), f32)], [], 0, 400_000, start_field, adjoint_source)
    fields = team_share(fields)
    first = lax.ppermute(local_inverse[0:SLOT], "col", [(3, 0)])
    third = lax.ppermute(local_inverse[2 * SLOT : 3 * SLOT], "col", [(3, 2)])
    diagonal = row_diagonal.reshape(1, OWN)
    code = weight_code.reshape(1, EXT)

    half = ((EXT, QUART), bf16)
    lam, pick, slots = call(
        start_kernel,
        [((ALLC, OWN), f32), ((OWN, SLOT), bf16), ((ALLC + 16, SLOT), f32)],
        [],
        100_000_000,
        1_000_000,
        *fields,
        coded,
        coarse_modes,
        coarse_inverse,
    )
    q_high, q_low = call(
        quarter_kernel,
        [half, half],
        [((32, QUART), f32), ((32, QUART), jnp.int32)],
        6_000_000_000,
        4_000_000,
        row_values,
        row_columns,
        diagonal,
        after=(lam,),
    )
    slots = team_pass(slots, -1)
    (slots,) = call(start_join_kernel, [((ALLC + 24, SLOT), f32)], [], 0, 80_000, slots, coded, after=(q_low,))
    slots = team_share(slots)
    c_high, c_low = call(
        chosen_kernel,
        [((EXT, SLOT), bf16), ((EXT, SLOT), bf16)],
        [((32, SLOT), f32), ((32, SLOT), jnp.int32), ((80, OWN), f32)],
        2_000_000_000,
        1_000_000,
        row_values,
        row_columns,
        diagonal,
        coded,
        pick,
        after=(slots[0],),
    )
    source_q, source_c, modes, inverse = call(
        source_kernel,
        [((ALLC, QUART), f32), ((ALLC, SLOT), f32), ((8, OWN), f32), ((8, SUBS * 8), f32)],
        [((ALLC, OWN), f32)],
        400_000_000,
        2_000_000,
        *fields,
        pick,
        coarse_modes,
        coarse_inverse,
    )
    w_high, w_low = pl.pallas_call(
        inverse_kernel,
        grid=(4,),
        out_shape=[jax.ShapeDtypeStruct((4, BLOCK, BLOCK), bf16)] * 2,
        in_specs=[
            pl.BlockSpec((BLOCK, QUART), lambda i: (0, i)),
            pl.BlockSpec((BLOCK, SLOT), lambda i: (0, 12 + i)),
            pl.BlockSpec((1, QUART), lambda i: (0, i)),
            pl.BlockSpec((1, SLOT), lambda i: (0, 12 + i)),
        ],
        out_specs=[pl.BlockSpec((1, BLOCK, BLOCK), lambda i: (i, 0, 0))] * 2,
        compiler_params=pltpu.CompilerParams(vmem_limit_bytes=12 << 20),
        cost_estimate=pl.CostEstimate(flops=4_000_000_000, bytes_accessed=8_000_000, transcendentals=0),
    )(local_inverse, local_inverse, code, code)
    m_high, m_low = call(
        margin_kernel,
        [((4, BLOCK, SLOT), bf16), ((4, BLOCK, SLOT), bf16)],
        [],
        1_000_000_000,
        3_000_000,
        first,
        third,
        code,
    )

    small = 600_000_000
    piece = ((ALLC, SLOT), f32)
    for iteration in range(ITERS):
        last = iteration == ITERS - 1
        operator = (q_high, q_low, c_high, c_low, source_q, source_c)
        if iteration == 0:
            quarter, send = call(
                first_residual_kernel,
                [((ALLC, QUART), f32), piece],
                [((4, ALLC, SLOT), f32)],
                small,
                5_000_000,
                lam,
                *slots,
                *operator,
            )
            spread, margin_modes, near = call(
                lists_kernel,
                [((BLOCK, OWN), bf16), ((4, 8, SLOT), f32), ((5, 8, 256), f32)],
                [],
                10_000_000,
                2_000_000,
                *slots,
                coarse_inverse,
            )
        else:
            quarter, send, lam = call(
                residual_kernel,
                [((ALLC, QUART), f32), piece, ((ALLC, OWN), f32)],
                [((4, ALLC, SLOT), f32), ((4, ALLC, 128), f32)],
                small,
                5_000_000,
                lam,
                *slots,
                *operator,
                modes,
                margin_modes,
                near,
            )
        (block,) = call(
            residual_join_kernel, [((ALLC, BLOCK), f32)], [], 0, 260_000, quarter, team_pass(send, -1)
        )
        blocks = team_share(block)
        solved, send_a, send_b, message = call(
            solve_kernel,
            [((ALLC, BLOCK), f32), piece, piece, ((8, 128), f32)],
            [((4, ALLC, BLOCK), f32)],
            small,
            5_000_000,
            *blocks,
            w_high,
            w_low,
            m_high,
            m_low,
            modes,
        )
        got = margin_pass(send_a, send_b, not last)
        if not last:
            odd = coarse_pass(message, 1, 1)
            (part,) = call(
                solve_join_kernel, [((ALLC + 8, PART), f32)], [], 0, 400_000, solved, *got, message, odd
            )
            lam, send, entries = call(
                update_kernel,
                [((ALLC, OWN), f32), piece, ((32, 128), f32)],
                [((4, ALLC, PART), f32)],
                small,
                3_000_000,
                *team_share(part),
                lam,
                spread,
                pick,
            )
            send = team_pass(send, -1)
            even, odd = coarse_pass(entries, 8, 0), coarse_pass(entries, 8, 1)
            (slots,) = call(
                update_join_kernel, [((2 * ALLC, SLOT), f32)], [], 0, 130_000, send, entries, even, odd
            )
            slots = team_share(slots)
        else:
            (everyone,) = call(
                entries_kernel,
                [((SUBS, 8, 128), f32)],
                [],
                10_000_000,
                700_000,
                *blocks,
                modes,
                after=tuple(got),
            )
            coarse_rhs = lax.all_to_all(everyone, "sub", 0, 0).reshape(SUBS * 8, 128)
            parts = call(
                final_join_kernel,
                [((COLS, PART), f32)] * 4,
                [((ALLC, PART), f32)],
                0,
                400_000,
                solved,
                *got,
            )
            parts = [parts[0]] + [step_pass(parts[step], step) for step in (1, 2, 3)]
            (values,) = call(
                final_kernel,
                [((COLS, OWN), f32)],
                [((4, COLS, PART), f32), ((128, 8), f32)],
                small,
                3_000_000,
                *parts,
                lam,
                spread,
                modes,
                inverse,
                coarse_rhs,
            )
    return values


def solution(mesh):
    return jax.shard_map(
        local,
        mesh=mesh,
        in_specs=(
            P("col", "sub"),
            P("col", "sub"),
            P("sub"),
            P(None, "sub"),
            P(None, "sub"),
            P("sub"),
            P("sub", None),
            P("sub", None, None),
            P(("sub", "col"), None),
            P(None, "sub"),
            P("sub", None),
        ),
        out_specs=P("col", "sub"),
        check_vma=False,
    )
```

```python
import functools
import jax
import jax.numpy as jnp
from jax import lax
from jax.experimental import pallas as pl
from jax.experimental.pallas import tpu as pltpu
from jax.sharding import PartitionSpec as P

ITERS = 3
OWN = 1536
EXT = 2048
SLOT = 128
QUART = 384
BLOCK = 512
PART = 640
TERMS = 26
MODES = 4
SUBS = 64
TEAM = 4
COLS = 16
ALLC = 64

direction_steps = (-2, -1, 1, 2)
damping = 0.7
margin_holder = (1, 0, 2, 3)
highest = lax.Precision.HIGHEST
f32 = jnp.float32
bf16 = jnp.bfloat16
contract_last = (((1,), (1,)), ((), ()))
contract_first = (((0,), (0,)), ((), ()))


def source_of(member, step):
    return lax.rem(member - step + TEAM, TEAM)


def split(x):
    high = x.astype(bf16)
    low = (x - high.astype(f32)).astype(bf16)
    return high, low


def dot(a, b):
    return jnp.dot(a, b, preferred_element_type=f32)


def dot3(x, w_high, w_low):
    rows = x.shape[0]
    high, low = split(x)
    both = dot(jnp.concatenate([high, low], axis=0), w_high)
    return both[:rows] + both[rows:] + dot(high, w_low)


def dot2(x, ones):
    rows = x.shape[0]
    high, low = split(x)
    both = dot(jnp.concatenate([high, low], axis=0), ones)
    return both[:rows] + both[rows:]


def row_list(coded):
    return (coded + 0.5).astype(jnp.int32) - 1


def dot_exact(x, ones):
    rows = x.shape[0]
    high, rest = split(x)
    low = x - high.astype(f32)
    low = (low - rest.astype(f32)).astype(bf16)
    parts = dot(jnp.concatenate([high, rest, low], axis=0), ones)
    return (parts[2 * rows :] + parts[rows : 2 * rows]) + parts[:rows]


def opening_kernel(field, source, count, rows, fields, coded, counts, lists, sems):
    copies = [
        pltpu.make_async_copy(count, counts, sems.at[0]),
        pltpu.make_async_copy(rows, lists, sems.at[1]),
        pltpu.make_async_copy(field, fields.at[0:COLS], sems.at[2]),
        pltpu.make_async_copy(source, fields.at[COLS : 2 * COLS], sems.at[3]),
    ]
    for copy in copies:
        copy.start()
    copies[0].wait()
    copies[1].wait()
    me = lax.axis_index("col")
    place = lax.broadcasted_iota(jnp.int32, (1, TEAM), 1)
    live = jnp.sum(jnp.where(place == me, counts[...], 0), axis=1, keepdims=True)
    index = lax.broadcasted_iota(jnp.int32, (1, SLOT), 1)
    coded[...] = jnp.where(index < live, lists[0, pl.ds(me, 1), :] + 1, 0).astype(f32)
    copies[2].wait()
    copies[3].wait()


def start_kernel(x0, x1, x2, x3, coded, modes, inverse, lam, pick, send):
    me = lax.axis_index("col")
    wanted = row_list(coded[...])
    for step, x in enumerate((x0, x1, x2, x3)):
        rows = pl.ds(pl.multiple_of(COLS * source_of(me, step), COLS), COLS)
        lam[rows, :] = x[0:COLS, :]
    for n in range(12):
        spot = lax.broadcasted_iota(jnp.int32, (128, SLOT), 0) + 128 * n
        pick[128 * n : 128 * n + 128, :] = (spot == wanted).astype(f32).astype(bf16)
    send[0:ALLC, :] = dot2(lam[...], pick[...])
    send[ALLC : ALLC + MODES, :] = jnp.dot(
        modes[...], pick[...].astype(f32), precision=highest, preferred_element_type=f32
    )
    send[ALLC + MODES : ALLC + 8, :] = jnp.zeros((MODES, SLOT), f32)
    send[ALLC + 8 : ALLC + 8 + MODES, :] = inverse[:, 0:128]
    send[ALLC + 8 + MODES : ALLC + 16, :] = inverse[:, 128:256]


def start_join_kernel(got, coded, out):
    out[0 : ALLC + 16, :] = got[...]
    out[ALLC + 16 :, :] = jnp.broadcast_to(coded[...], (8, SLOT))


def source_kernel(x0, x1, x2, x3, pick, modes, inverse, quarter, chosen, modes_out, inv_out, scr):
    me = lax.axis_index("col")
    for step, x in enumerate((x0, x1, x2, x3)):
        rows = pl.ds(pl.multiple_of(COLS * source_of(me, step), COLS), COLS)
        scr[rows, :] = x[COLS:, :]
    for j in range(3):
        at = pl.ds(pl.multiple_of(QUART * me + 128 * j, 128), 128)
        quarter[:, 128 * j : 128 * j + 128] = scr[:, at]
    chosen[...] = dot_exact(scr[...], pick[...])
    modes_out[...] = jnp.zeros(modes_out.shape, f32)
    modes_out[0:MODES, :] = modes[...]
    width = SUBS * MODES
    at = lax.broadcasted_iota(jnp.int32, (width, SUBS * 8), 0)
    to = lax.broadcasted_iota(jnp.int32, (width, SUBS * 8), 1)
    spread = jnp.logical_and(at // MODES == to // 8, lax.rem(at, MODES) == lax.rem(to, 8)).astype(f32)
    inv_out[...] = jnp.zeros(inv_out.shape, f32)
    inv_out[0:MODES, :] = jnp.dot(inverse[...], spread, precision=highest, preferred_element_type=f32)


def lists_kernel(s0, s1, s2, s3, inverse, spread, margin_modes, near):
    me = lax.axis_index("col")
    width = SUBS * MODES
    at = lax.broadcasted_iota(jnp.int32, (width, width), 0)
    to = lax.broadcasted_iota(jnp.int32, (width, width), 1)
    other = lax.bitwise_xor(to // MODES, lax.axis_index("sub").astype(jnp.int32))
    turn = (at == MODES * other + lax.rem(to, MODES)).astype(f32)
    near[...] = jnp.zeros(near.shape, f32)

    def turned(left, right):
        return jnp.dot(
            jnp.concatenate([left, right], axis=1), turn, precision=highest, preferred_element_type=f32
        )

    near[4, 0:MODES, :] = turned(inverse[:, 0:128], inverse[:, 128:256])
    for step, s in enumerate((s0, s1, s2, s3)):
        source = source_of(me, step)
        margin_modes[source] = s[ALLC : ALLC + 8, :]
        near[source, 0:MODES, :] = turned(s[ALLC + 8 : ALLC + 12, :], s[ALLC + 12 : ALLC + 16, :])
        at = pl.multiple_of(SLOT * source, SLOT)
        coded = jnp.concatenate([s[ALLC + 16 :, :], jnp.zeros((120, SLOT), f32)], axis=0).T
        wanted = jnp.broadcast_to(row_list(coded[:, 0:1]), (SLOT, 128))
        for n in range(12):
            spot = lax.broadcasted_iota(jnp.int32, (SLOT, 128), 1) + 128 * n
            spread[pl.ds(at, SLOT), 128 * n : 128 * n + 128] = (spot == wanted).astype(f32).astype(bf16)


def dense(col, val, high, low, lanes, start, tiles):
    def body(number, carry):
        tile = number + start
        b, j = tile // 8, lax.rem(tile // 2, 4)
        first = jnp.where(j < 3, QUART * b + 128 * j, OWN + SLOT * b) + 64 * lax.rem(tile, 2)
        rows = pl.ds(pl.multiple_of(number * 64, 64), 64)
        spot = lax.broadcasted_iota(jnp.int32, (64, 128), 0) + first
        for lane in range(lanes):
            to = slice(128 * lane, 128 * lane + 128)
            total = jnp.zeros((64, 128), f32)
            for term in range(TERMS + 1):
                total = total + jnp.where(spot == col[term : term + 1, to], val[term : term + 1, to], 0.0)
            high[rows, to], low[rows, to] = split(total)
        return carry

    lax.fori_loop(0, tiles, body, 0)


def quarter_terms(values, columns, diagonal, val, col):
    me = lax.axis_index("col")
    for j in range(3):
        at = pl.ds(pl.multiple_of(QUART * me + 128 * j, 128), 128)
        to = slice(128 * j, 128 * j + 128)
        val[0:TERMS, to] = values[:, at]
        col[0:TERMS, to] = columns[:, at]
        val[TERMS : TERMS + 1, to] = diagonal[:, at]
        col[TERMS : TERMS + 1, to] = lax.broadcasted_iota(jnp.int32, (1, 128), 1) + (QUART * me + 128 * j)


def first_half_kernel(values, columns, diagonal, high, low, val, col):
    quarter_terms(values, columns, diagonal, val, col)
    dense(col, val, high, low, 3, 0, 16)


def second_half_kernel(values, columns, diagonal, high, low, val, col):
    quarter_terms(values, columns, diagonal, val, col)
    dense(col, val, high, low, 3, 16, 16)


def chosen_kernel(values, columns, diagonal, coded, pick, high, low, val, col, rows):
    rows[...] = jnp.zeros(rows.shape, f32)
    rows[0:TERMS, :] = values[...]
    rows[32 : 32 + TERMS, :] = columns[...].astype(f32)
    rows[64:65, :] = diagonal[...]
    found = dot_exact(rows[...], pick[...])
    val[0:TERMS, :] = found[0:TERMS]
    col[0:TERMS, :] = (found[32 : 32 + TERMS] + 0.5).astype(jnp.int32)
    val[TERMS : TERMS + 1, :] = found[64:65]
    col[TERMS : TERMS + 1, :] = row_list(coded[...])
    dense(col, val, high, low, 1, 0, 32)


def inverse_kernel(owned, margin, code_owned, code_margin, high, low):
    for j in range(4):
        if j < 3:
            lanes = slice(128 * j, 128 * j + 128)
            tile, code = owned[:, lanes], code_owned[:, lanes]
        else:
            tile, code = margin[...], code_margin[...]
        first, second = split((tile * (1.0 / (1.0 + code.astype(f32)))).T)
        high[0, 128 * j : 128 * j + 128, :] = first
        low[0, 128 * j : 128 * j + 128, :] = second


def residual_of(lam, scr, q_pairs, c_high, c_low, source_q, source_c, quarter, slots):
    owned = jnp.zeros((ALLC, QUART), f32)
    chosen = jnp.zeros((ALLC, SLOT), f32)
    for b in range(4):
        x = jnp.concatenate([lam[:, QUART * b : QUART * b + QUART], scr[b]], axis=1)
        rows = slice(BLOCK * b, BLOCK * b + BLOCK)
        chosen = chosen + dot3(x, c_high[rows, :], c_low[rows, :])
        rows = slice(BLOCK * (b % 2), BLOCK * (b % 2) + BLOCK)
        high, low = q_pairs[2 * (b // 2) : 2 * (b // 2) + 2]
        owned = owned + dot3(x, high[rows, :], low[rows, :])
    quarter[...] = source_q[...] - owned
    slots[...] = source_c[...] - chosen


def margin_kernel(first, third, code_owned, high, low):
    mine = lax.axis_index("col") == 0
    for b in range(4):
        for j in range(4):
            if j < 3:
                n = QUART * b + 128 * j
            else:
                n = OWN + SLOT * b
            lanes = slice(n, n + 128)
            tile = jnp.where(mine, first[:, lanes], third[:, lanes])
            code = code_owned[:, lanes]
            upper, lower = split((tile * (1.0 / (1.0 + code.astype(f32)))).T)
            high[b, 128 * j : 128 * j + 128, :] = upper
            low[b, 128 * j : 128 * j + 128, :] = lower


def first_residual_kernel(
    lam, s0, s1, s2, s3, qa, qb, qc, qd, c_high, c_low, source_q, source_c, quarter, slots, scr
):
    me = lax.axis_index("col")
    for step, s in enumerate((s0, s1, s2, s3)):
        scr[source_of(me, step)] = s[0:ALLC, :]
    residual_of(lam, scr, (qa, qb, qc, qd), c_high, c_low, source_q, source_c, quarter, slots)


def dot_pair(x, w):
    x_high, x_low = split(x)
    w_high, w_low = split(w)
    return dot(x_high, w_high) + (dot(x_low, w_high) + dot(x_high, w_low))


def residual_kernel(
    lam, s0, s1, s2, s3, qa, qb, qc, qd, c_high, c_low, source_q, source_c,
    modes, margin_modes, near, quarter, slots, out, scr, rhs,
):
    me = lax.axis_index("col")
    for step, s in enumerate((s0, s1, s2, s3)):
        pair = s[ALLC:, :]
        rhs[source_of(me, step), 0:32, :] = pair
        rhs[source_of(me, step), 32:64, :] = pltpu.roll(pair, 64, 1)
        scr[source_of(me, step)] = s[0:ALLC, :]
    coarse = dot_pair(near[...].reshape(40, 256), rhs[...].reshape(256, 128))
    coarse = jnp.concatenate([coarse, jnp.zeros((88, 128), f32)], axis=0).T[:ALLC]

    def lift(number, shape):
        return damping * dot_pair(coarse[:, 8 * number : 8 * number + 8], shape)

    for b in range(4):
        scr[b] = scr[b] + lift(b, margin_modes[b])
    for b in range(3):
        to = slice(BLOCK * b, BLOCK * b + BLOCK)
        out[:, to] = lam[:, to] + lift(4, modes[:, to])
    residual_of(out, scr, (qa, qb, qc, qd), c_high, c_low, source_q, source_c, quarter, slots)


def residual_join_kernel(quarter, got, out):
    out[:, 0:QUART] = quarter[...]
    out[:, QUART:] = got[...]


def solve_kernel(x0, x1, x2, x3, high, low, m_high, m_low, modes, solved, send_a, send_b, message, scr):
    me = lax.axis_index("col")
    for step, x in enumerate((x0, x1, x2, x3)):
        scr[source_of(me, step)] = x[...]
    total = jnp.zeros((ALLC, BLOCK), f32)
    extra = jnp.zeros((ALLC, SLOT), f32)
    rhs = jnp.zeros((8, ALLC), f32)
    for b in range(4):
        x = scr[b]
        extra = extra + dot3(x, m_high[b], m_low[b])
        total = total + dot3(x, high[b], low[b])
        rhs = rhs + lax.dot_general(
            modes[:, QUART * b : QUART * b + QUART],
            x[:, :QUART],
            contract_last,
            precision=highest,
            preferred_element_type=f32,
        )
    rhs = jnp.concatenate([rhs, jnp.zeros((8, 128 - ALLC), f32)], axis=1)
    below = jnp.concatenate([rhs, jnp.zeros((ALLC - 8, 128), f32)], axis=0)
    solved[...] = total
    send_a[...] = jnp.where(me == 3, total[:, 3 * SLOT :], extra)
    send_b[...] = jnp.where(me == 3, total[:, SLOT : 2 * SLOT], below)
    message[...] = rhs


def coarse_part(inverse, coarse_rhs):
    coarse = jnp.dot(inverse[...], coarse_rhs[...], precision=highest, preferred_element_type=f32)
    return coarse.T


def field_part(lam, solved, back, spread, coarse, modes):
    lifted = jnp.dot(coarse, modes, precision=highest, preferred_element_type=f32)
    return lam + damping * (solved + dot2(back, spread) + lifted)


def entries_kernel(x0, x1, x2, x3, modes, everyone):
    me = lax.axis_index("col")
    rhs = jnp.zeros((8, ALLC), f32)
    for step, x in enumerate((x0, x1, x2, x3)):
        at = pl.ds(pl.multiple_of(QUART * source_of(me, step), 128), QUART)
        rhs = rhs + lax.dot_general(
            modes[:, at], x[:, 0:QUART], contract_last, precision=highest, preferred_element_type=f32
        )
    rhs = jnp.concatenate([rhs, jnp.zeros((8, 128 - ALLC), f32)], axis=1)
    everyone[...] = jnp.broadcast_to(rhs[None], everyone.shape)


def solve_join_kernel(solved, got_a, got_b, message, odd, out):
    first = lax.axis_index("col") == 0
    out[0:ALLC, 0:BLOCK] = solved[...]
    out[0:ALLC, BLOCK:] = jnp.where(first, got_b[...], got_a[...])
    out[ALLC:, :] = jnp.zeros((8, PART), f32)
    out[ALLC : ALLC + MODES, 0:128] = jnp.where(first, message[0:MODES, :], got_b[0:MODES, :])
    out[ALLC + MODES : ALLC + 8, 0:128] = odd[0:MODES, :]


def final_join_kernel(solved, got_a, got_b, p0, p1, p2, p3, scr):
    me = lax.axis_index("col")
    scr[:, 0:BLOCK] = solved[...]
    scr[:, BLOCK:] = jnp.where(me == 0, got_b[...], got_a[...])
    for step, p in enumerate((p0, p1, p2, p3)):
        p[...] = scr[pl.ds(pl.multiple_of(COLS * lax.rem(me + step, TEAM), COLS), COLS), :]


def update_kernel(x0, x1, x2, x3, lam, spread, pick, out, slots, entries, scr):
    me = lax.axis_index("col")
    for step, x in enumerate((x0, x1, x2, x3)):
        source = source_of(me, step)
        scr[source] = x[0:ALLC, :]
        entries[pl.ds(pl.multiple_of(8 * source, 8), 8), :] = x[ALLC:, 0:128]
    back = jnp.concatenate([scr[b, :, BLOCK:] for b in margin_holder], axis=1)
    send = jnp.zeros((ALLC, SLOT), f32)
    for b in range(3):
        to = slice(BLOCK * b, BLOCK * b + BLOCK)
        fresh = lam[:, to] + damping * (scr[b, :, :BLOCK] + dot2(back, spread[:, to]))
        out[:, to] = fresh
        send = send + dot2(fresh, pick[to, :])
    slots[...] = send


def update_join_kernel(got, entries, even, odd, out):
    first = lax.axis_index("col") == 0
    out[0:ALLC, :] = got[...]
    left = jnp.where(first, entries[...], even[...])
    place = lax.broadcasted_iota(jnp.int32, left.shape, 1)
    out[ALLC:, :] = jnp.where(place < ALLC, left, pltpu.roll(odd[...], 64, 1))


def final_kernel(x0, x1, x2, x3, lam, spread, modes, inverse, coarse_rhs, out, scr, across):
    me = lax.axis_index("col")
    for step, x in enumerate((x0, x1, x2, x3)):
        scr[source_of(me, step)] = x[...]
    rows = pl.ds(pl.multiple_of(COLS * me, COLS), COLS)
    back = jnp.concatenate([scr[b, :, BLOCK:] for b in margin_holder], axis=1)
    across[...] = coarse_part(inverse, coarse_rhs)
    coarse = across[rows, :]
    for b in range(3):
        to = slice(BLOCK * b, BLOCK * b + BLOCK)
        out[:, to] = field_part(lam[rows, to], scr[b, :, :BLOCK], back, spread[:, to], coarse, modes[:, to])


def call(kernel, outs, scratch, flops, nbytes, *args, after=(), limit=6 << 20):
    taken = len(args)

    def body(*refs):
        kernel(*refs[:taken], *refs[taken + len(after) :])

    return pl.pallas_call(
        body,
        out_shape=[jax.ShapeDtypeStruct(shape, dtype) for shape, dtype in outs],
        in_specs=[pl.BlockSpec(memory_space=pltpu.VMEM)] * taken
        + [pl.BlockSpec(memory_space=pl.ANY)] * len(after),
        out_specs=[pl.BlockSpec(memory_space=pltpu.VMEM)] * len(outs),
        scratch_shapes=[pltpu.VMEM(shape, dtype) for shape, dtype in scratch],
        compiler_params=pltpu.CompilerParams(vmem_limit_bytes=limit),
        cost_estimate=pl.CostEstimate(flops=flops, bytes_accessed=nbytes, transcendentals=0),
        name=kernel.__name__,
    )(*args, *after)


def team_pass(x, sign):
    pairs = []
    for s in range(SUBS):
        for d, step in enumerate(direction_steps):
            t = s + sign * step
            if 0 <= t < SUBS:
                pairs.append((s * TEAM + d, t * TEAM + d))
    return lax.ppermute(x, ("sub", "col"), pairs)


def margin_pass(send_a, send_b, with_coarse):
    first, second = [], []
    for s in range(SUBS):
        for d, source in ((0, 0), (2, 2), (3, 3), (1, 3)):
            t = s + direction_steps[d]
            if 0 <= t < SUBS:
                pair = (s * TEAM + source, t * TEAM + margin_holder[d])
                (second if d == 1 else first).append(pair)
        if with_coarse:
            for c in (1, 2, 3):
                second.append(((s ^ (2 * c)) * TEAM + c - 1, s * TEAM + c))
    axes = ("sub", "col")
    return lax.ppermute(send_a, axes, first), lax.ppermute(send_b, axes, second)


def coarse_pass(x, width, odd):
    pairs = [
        ((s ^ (width * (2 * c + odd))) * TEAM + c, s * TEAM + c)
        for s in range(SUBS)
        for c in range(TEAM)
        if 2 * c + odd > 0
    ]
    return lax.ppermute(x, ("sub", "col"), pairs)


def step_pass(x, step):
    return lax.ppermute(x, "col", [(i, (i + step) % TEAM) for i in range(TEAM)])


def team_share(x):
    return [x] + [step_pass(x, step) for step in (1, 2, 3)]


def local(
    adjoint_source,
    start_field,
    row_diagonal,
    row_values,
    row_columns,
    weight_code,
    slot_count,
    slot_rows,
    local_inverse,
    coarse_modes,
    coarse_inverse,
):
    fields, coded = pl.pallas_call(
        opening_kernel,
        out_shape=[jax.ShapeDtypeStruct((2 * COLS, OWN), f32), jax.ShapeDtypeStruct((1, SLOT), f32)],
        in_specs=[pl.BlockSpec(memory_space=pltpu.HBM)] * 4,
        out_specs=[pl.BlockSpec(memory_space=pltpu.VMEM)] * 2,
        scratch_shapes=[
            pltpu.VMEM((1, TEAM), jnp.int32),
            pltpu.VMEM((1, TEAM, SLOT), jnp.int32),
            pltpu.SemaphoreType.DMA((4,)),
        ],
        compiler_params=pltpu.CompilerParams(vmem_limit_bytes=60 << 20),
        cost_estimate=pl.CostEstimate(flops=0, bytes_accessed=400_000, transcendentals=0),
    )(start_field, adjoint_source, slot_count, slot_rows)
    coded = team_pass(coded, 1)
    fields = team_share(fields)
    first = lax.ppermute(local_inverse[0:SLOT], "col", [(3, 0)])
    third = lax.ppermute(local_inverse[2 * SLOT : 3 * SLOT], "col", [(3, 2)])
    diagonal = row_diagonal.reshape(1, OWN)
    code = weight_code.reshape(1, EXT)

    lam, pick, slots = call(
        start_kernel,
        [((ALLC, OWN), f32), ((OWN, SLOT), bf16), ((ALLC + 16, SLOT), f32)],
        [],
        100_000_000,
        1_000_000,
        *fields,
        coded,
        coarse_modes,
        coarse_inverse,
    )
    half = ((EXT // 2, QUART), bf16)
    terms = [((32, QUART), f32), ((32, QUART), jnp.int32)]
    q_pairs = call(
        first_half_kernel,
        [half, half],
        terms,
        3_000_000_000,
        3_000_000,
        row_values,
        row_columns,
        diagonal,
        after=(lam,),
    )
    slots = team_pass(slots, -1)
    (slots,) = call(start_join_kernel, [((ALLC + 24, SLOT), f32)], [], 0, 80_000, slots, coded, after=(q_pairs[0],))
    slots = team_share(slots)
    q_pairs += call(
        second_half_kernel,
        [half, half],
        terms,
        3_000_000_000,
        3_000_000,
        row_values,
        row_columns,
        diagonal,
        after=(slots[0],),
    )
    c_high, c_low = call(
        chosen_kernel,
        [((EXT, SLOT), bf16), ((EXT, SLOT), bf16)],
        [((32, SLOT), f32), ((32, SLOT), jnp.int32), ((80, OWN), f32)],
        2_000_000_000,
        1_000_000,
        row_values,
        row_columns,
        diagonal,
        coded,
        pick,
        after=(slots[0],),
    )
    source_q, source_c, modes, inverse = call(
        source_kernel,
        [((ALLC, QUART), f32), ((ALLC, SLOT), f32), ((8, OWN), f32), ((8, SUBS * 8), f32)],
        [((ALLC, OWN), f32)],
        400_000_000,
        2_000_000,
        *fields,
        pick,
        coarse_modes,
        coarse_inverse,
    )
    w_high, w_low = pl.pallas_call(
        inverse_kernel,
        grid=(4,),
        out_shape=[jax.ShapeDtypeStruct((4, BLOCK, BLOCK), bf16)] * 2,
        in_specs=[
            pl.BlockSpec((BLOCK, QUART), lambda i: (0, i)),
            pl.BlockSpec((BLOCK, SLOT), lambda i: (0, 12 + i)),
            pl.BlockSpec((1, QUART), lambda i: (0, i)),
            pl.BlockSpec((1, SLOT), lambda i: (0, 12 + i)),
        ],
        out_specs=[pl.BlockSpec((1, BLOCK, BLOCK), lambda i: (i, 0, 0))] * 2,
        compiler_params=pltpu.CompilerParams(vmem_limit_bytes=12 << 20),
        cost_estimate=pl.CostEstimate(flops=4_000_000_000, bytes_accessed=8_000_000, transcendentals=0),
    )(local_inverse, local_inverse, code, code)
    m_high, m_low = call(
        margin_kernel,
        [((4, BLOCK, SLOT), bf16), ((4, BLOCK, SLOT), bf16)],
        [],
        1_000_000_000,
        3_000_000,
        first,
        third,
        code,
    )

    small = 600_000_000
    piece = ((ALLC, SLOT), f32)
    for iteration in range(ITERS):
        last = iteration == ITERS - 1
        operator = (*q_pairs, c_high, c_low, source_q, source_c)
        if iteration == 0:
            quarter, send = call(
                first_residual_kernel,
                [((ALLC, QUART), f32), piece],
                [((4, ALLC, SLOT), f32)],
                small,
                5_000_000,
                lam,
                *slots,
                *operator,
            )
            spread, margin_modes, near = call(
                lists_kernel,
                [((BLOCK, OWN), bf16), ((4, 8, SLOT), f32), ((5, 8, 256), f32)],
                [],
                10_000_000,
                2_000_000,
                *slots,
                coarse_inverse,
            )
        else:
            quarter, send, lam = call(
                residual_kernel,
                [((ALLC, QUART), f32), piece, ((ALLC, OWN), f32)],
                [((4, ALLC, SLOT), f32), ((4, ALLC, 128), f32)],
                small,
                5_000_000,
                lam,
                *slots,
                *operator,
                modes,
                margin_modes,
                near,
            )
        (block,) = call(
            residual_join_kernel, [((ALLC, BLOCK), f32)], [], 0, 260_000, quarter, team_pass(send, -1)
        )
        blocks = team_share(block)
        solved, send_a, send_b, message = call(
            solve_kernel,
            [((ALLC, BLOCK), f32), piece, piece, ((8, 128), f32)],
            [((4, ALLC, BLOCK), f32)],
            small,
            5_000_000,
            *blocks,
            w_high,
            w_low,
            m_high,
            m_low,
            modes,
        )
        got = margin_pass(send_a, send_b, not last)
        if not last:
            odd = coarse_pass(message, 1, 1)
            (part,) = call(
                solve_join_kernel, [((ALLC + 8, PART), f32)], [], 0, 400_000, solved, *got, message, odd
            )
            lam, send, entries = call(
                update_kernel,
                [((ALLC, OWN), f32), piece, ((32, 128), f32)],
                [((4, ALLC, PART), f32)],
                small,
                3_000_000,
                *team_share(part),
                lam,
                spread,
                pick,
            )
            send = team_pass(send, -1)
            even, odd = coarse_pass(entries, 8, 0), coarse_pass(entries, 8, 1)
            (slots,) = call(
                update_join_kernel, [((ALLC + 32, SLOT), f32)], [], 0, 130_000, send, entries, even, odd
            )
            slots = team_share(slots)
        else:
            (everyone,) = call(
                entries_kernel,
                [((SUBS, 8, 128), f32)],
                [],
                10_000_000,
                700_000,
                *blocks,
                modes,
                after=tuple(got),
            )
            coarse_rhs = lax.all_to_all(everyone, "sub", 0, 0).reshape(SUBS * 8, 128)
            parts = call(
                final_join_kernel,
                [((COLS, PART), f32)] * 4,
                [((ALLC, PART), f32)],
                0,
                400_000,
                solved,
                *got,
            )
            parts = [parts[0]] + [step_pass(parts[step], step) for step in (1, 2, 3)]
            (values,) = call(
                final_kernel,
                [((COLS, OWN), f32)],
                [((4, COLS, PART), f32), ((128, 8), f32)],
                small,
                3_000_000,
                *parts,
                lam,
                spread,
                modes,
                inverse,
                coarse_rhs,
            )
    return values


def solution(mesh):
    return jax.shard_map(
        local,
        mesh=mesh,
        in_specs=(
            P("col", "sub"),
            P("col", "sub"),
            P("sub"),
            P(None, "sub"),
            P(None, "sub"),
            P("sub"),
            P("sub", None),
            P("sub", None, None),
            P(("sub", "col"), None),
            P(None, "sub"),
            P("sub", None),
        ),
        out_specs=P("col", "sub"),
        check_vma=False,
    )
```

```python
import functools
import jax
import jax.numpy as jnp
from jax import lax
from jax.experimental import pallas as pl
from jax.experimental.pallas import tpu as pltpu
from jax.sharding import PartitionSpec as P

ITERS = 3
OWN = 1536
EXT = 2048
SLOT = 128
QUART = 384
BLOCK = 512
PART = 640
TERMS = 26
MODES = 4
SUBS = 64
TEAM = 4
COLS = 16
ALLC = 64

direction_steps = (-2, -1, 1, 2)
damping = 0.7
margin_holder = (1, 0, 2, 3)
team_steps = (0, 1, 3, 2)
highest = lax.Precision.HIGHEST
f32 = jnp.float32
bf16 = jnp.bfloat16
contract_last = (((1,), (1,)), ((), ()))
contract_first = (((0,), (0,)), ((), ()))


def source_of(member, step):
    return lax.rem(member - step + TEAM, TEAM)


def split(x):
    high = x.astype(bf16)
    low = (x - high.astype(f32)).astype(bf16)
    return high, low


def dot(a, b):
    return jnp.dot(a, b, preferred_element_type=f32)


def dot3(x, w_high, w_low):
    rows = x.shape[0]
    high, low = split(x)
    both = dot(jnp.concatenate([high, low], axis=0), w_high)
    return both[:rows] + both[rows:] + dot(high, w_low)


def dot2(x, ones):
    rows = x.shape[0]
    high, low = split(x)
    both = dot(jnp.concatenate([high, low], axis=0), ones)
    return both[:rows] + both[rows:]


def row_list(coded):
    return (coded + 0.5).astype(jnp.int32) - 1


def dot_exact(x, ones):
    rows = x.shape[0]
    high, rest = split(x)
    low = x - high.astype(f32)
    low = (low - rest.astype(f32)).astype(bf16)
    parts = dot(jnp.concatenate([high, rest, low], axis=0), ones)
    return (parts[2 * rows :] + parts[rows : 2 * rows]) + parts[:rows]


def opening_kernel(field, source, count, rows, fields, coded, counts, lists, sems):
    copies = [
        pltpu.make_async_copy(count, counts, sems.at[0]),
        pltpu.make_async_copy(rows, lists, sems.at[1]),
        pltpu.make_async_copy(field, fields.at[0:COLS], sems.at[2]),
        pltpu.make_async_copy(source, fields.at[COLS : 2 * COLS], sems.at[3]),
    ]
    for copy in copies:
        copy.start()
    copies[0].wait()
    copies[1].wait()
    me = lax.axis_index("col")
    place = lax.broadcasted_iota(jnp.int32, (1, TEAM), 1)
    live = jnp.sum(jnp.where(place == me, counts[...], 0), axis=1, keepdims=True)
    index = lax.broadcasted_iota(jnp.int32, (1, SLOT), 1)
    coded[...] = jnp.where(index < live, lists[0, pl.ds(me, 1), :] + 1, 0).astype(f32)
    copies[2].wait()
    copies[3].wait()


def start_kernel(x0, x1, x2, x3, coded, modes, inverse, lam, pick, send):
    me = lax.axis_index("col")
    wanted = row_list(coded[...])
    for step, x in zip(team_steps, (x0, x1, x2, x3)):
        rows = pl.ds(pl.multiple_of(COLS * source_of(me, step), COLS), COLS)
        lam[rows, :] = x[0:COLS, :]
    for n in range(12):
        spot = lax.broadcasted_iota(jnp.int32, (128, SLOT), 0) + 128 * n
        pick[128 * n : 128 * n + 128, :] = (spot == wanted).astype(f32).astype(bf16)
    send[0:ALLC, :] = dot2(lam[...], pick[...])
    send[ALLC : ALLC + MODES, :] = jnp.dot(
        modes[...], pick[...].astype(f32), precision=highest, preferred_element_type=f32
    )
    send[ALLC + MODES : ALLC + 8, :] = jnp.zeros((MODES, SLOT), f32)
    send[ALLC + 8 : ALLC + 8 + MODES, :] = inverse[:, 0:128]
    send[ALLC + 8 + MODES : ALLC + 16, :] = inverse[:, 128:256]


def start_join_kernel(got, coded, out):
    out[0 : ALLC + 16, :] = got[...]
    out[ALLC + 16 :, :] = jnp.broadcast_to(coded[...], (8, SLOT))


def source_kernel(x0, x1, x2, x3, pick, modes, inverse, quarter, chosen, modes_out, inv_out, scr):
    me = lax.axis_index("col")
    for step, x in zip(team_steps, (x0, x1, x2, x3)):
        rows = pl.ds(pl.multiple_of(COLS * source_of(me, step), COLS), COLS)
        scr[rows, :] = x[COLS:, :]
    for j in range(3):
        at = pl.ds(pl.multiple_of(QUART * me + 128 * j, 128), 128)
        quarter[:, 128 * j : 128 * j + 128] = scr[:, at]
    chosen[...] = dot_exact(scr[...], pick[...])
    modes_out[...] = jnp.zeros(modes_out.shape, f32)
    modes_out[0:MODES, :] = modes[...]
    width = SUBS * MODES
    at = lax.broadcasted_iota(jnp.int32, (width, SUBS * 8), 0)
    to = lax.broadcasted_iota(jnp.int32, (width, SUBS * 8), 1)
    spread = jnp.logical_and(at // MODES == to // 8, lax.rem(at, MODES) == lax.rem(to, 8)).astype(f32)
    inv_out[...] = jnp.zeros(inv_out.shape, f32)
    inv_out[0:MODES, :] = jnp.dot(inverse[...], spread, precision=highest, preferred_element_type=f32)


def lists_kernel(s0, s1, s2, s3, inverse, spread, margin_modes, near):
    me = lax.axis_index("col")
    width = SUBS * MODES
    at = lax.broadcasted_iota(jnp.int32, (width, width), 0)
    to = lax.broadcasted_iota(jnp.int32, (width, width), 1)
    other = lax.bitwise_xor(to // MODES, lax.axis_index("sub").astype(jnp.int32))
    turn = (at == MODES * other + lax.rem(to, MODES)).astype(f32)
    near[...] = jnp.zeros(near.shape, f32)

    def turned(left, right):
        return jnp.dot(
            jnp.concatenate([left, right], axis=1), turn, precision=highest, preferred_element_type=f32
        )

    near[4, 0:MODES, :] = turned(inverse[:, 0:128], inverse[:, 128:256])
    for step, s in zip(team_steps, (s0, s1, s2, s3)):
        source = source_of(me, step)
        margin_modes[source] = s[ALLC : ALLC + 8, :]
        near[source, 0:MODES, :] = turned(s[ALLC + 8 : ALLC + 12, :], s[ALLC + 12 : ALLC + 16, :])
        at = pl.multiple_of(SLOT * source, SLOT)
        coded = jnp.concatenate([s[ALLC + 16 :, :], jnp.zeros((120, SLOT), f32)], axis=0).T
        wanted = jnp.broadcast_to(row_list(coded[:, 0:1]), (SLOT, 128))
        for n in range(12):
            spot = lax.broadcasted_iota(jnp.int32, (SLOT, 128), 1) + 128 * n
            spread[pl.ds(at, SLOT), 128 * n : 128 * n + 128] = (spot == wanted).astype(f32).astype(bf16)


def dense(col, val, high, low, lanes, start, tiles):
    def body(number, carry):
        tile = number + start
        b, j = tile // 8, lax.rem(tile // 2, 4)
        first = jnp.where(j < 3, QUART * b + 128 * j, OWN + SLOT * b) + 64 * lax.rem(tile, 2)
        rows = pl.ds(pl.multiple_of(number * 64, 64), 64)
        spot = lax.broadcasted_iota(jnp.int32, (64, 128), 0) + first
        for lane in range(lanes):
            to = slice(128 * lane, 128 * lane + 128)
            total = jnp.zeros((64, 128), f32)
            for term in range(TERMS + 1):
                total = total + jnp.where(spot == col[term : term + 1, to], val[term : term + 1, to], 0.0)
            high[rows, to], low[rows, to] = split(total)
        return carry

    lax.fori_loop(0, tiles, body, 0)


def quarter_terms(values, columns, diagonal, val, col):
    me = lax.axis_index("col")
    for j in range(3):
        at = pl.ds(pl.multiple_of(QUART * me + 128 * j, 128), 128)
        to = slice(128 * j, 128 * j + 128)
        val[0:TERMS, to] = values[:, at]
        col[0:TERMS, to] = columns[:, at]
        val[TERMS : TERMS + 1, to] = diagonal[:, at]
        col[TERMS : TERMS + 1, to] = lax.broadcasted_iota(jnp.int32, (1, 128), 1) + (QUART * me + 128 * j)


def first_half_kernel(values, columns, diagonal, high, low, val, col):
    quarter_terms(values, columns, diagonal, val, col)
    dense(col, val, high, low, 3, 0, 16)


def second_half_kernel(values, columns, diagonal, high, low, val, col):
    quarter_terms(values, columns, diagonal, val, col)
    dense(col, val, high, low, 3, 16, 16)


def chosen_kernel(values, columns, diagonal, coded, pick, high, low, val, col, rows):
    rows[...] = jnp.zeros(rows.shape, f32)
    rows[0:TERMS, :] = values[...]
    rows[32 : 32 + TERMS, :] = columns[...].astype(f32)
    rows[64:65, :] = diagonal[...]
    found = dot_exact(rows[...], pick[...])
    val[0:TERMS, :] = found[0:TERMS]
    col[0:TERMS, :] = (found[32 : 32 + TERMS] + 0.5).astype(jnp.int32)
    val[TERMS : TERMS + 1, :] = found[64:65]
    col[TERMS : TERMS + 1, :] = row_list(coded[...])
    dense(col, val, high, low, 1, 0, 32)


def inverse_kernel(owned, margin, code_owned, code_margin, high, low):
    for j in range(4):
        if j < 3:
            lanes = slice(128 * j, 128 * j + 128)
            tile, code = owned[:, lanes], code_owned[:, lanes]
        else:
            tile, code = margin[...], code_margin[...]
        first, second = split((tile * (1.0 / (1.0 + code.astype(f32)))).T)
        high[0, 128 * j : 128 * j + 128, :] = first
        low[0, 128 * j : 128 * j + 128, :] = second


def residual_of(lam, scr, q_pairs, c_high, c_low, source_q, source_c, quarter, slots):
    owned = jnp.zeros((ALLC, QUART), f32)
    chosen = jnp.zeros((ALLC, SLOT), f32)
    for b in range(4):
        x = jnp.concatenate([lam[:, QUART * b : QUART * b + QUART], scr[b]], axis=1)
        rows = slice(BLOCK * b, BLOCK * b + BLOCK)
        chosen = chosen + dot3(x, c_high[rows, :], c_low[rows, :])
        rows = slice(BLOCK * (b % 2), BLOCK * (b % 2) + BLOCK)
        high, low = q_pairs[2 * (b // 2) : 2 * (b // 2) + 2]
        owned = owned + dot3(x, high[rows, :], low[rows, :])
    quarter[...] = source_q[...] - owned
    slots[...] = source_c[...] - chosen


def margin_kernel(first, third, code_owned, high, low):
    mine = lax.axis_index("col") == 0
    for b in range(4):
        for j in range(4):
            if j < 3:
                n = QUART * b + 128 * j
            else:
                n = OWN + SLOT * b
            lanes = slice(n, n + 128)
            tile = jnp.where(mine, first[:, lanes], third[:, lanes])
            code = code_owned[:, lanes]
            upper, lower = split((tile * (1.0 / (1.0 + code.astype(f32)))).T)
            high[b, 128 * j : 128 * j + 128, :] = upper
            low[b, 128 * j : 128 * j + 128, :] = lower


def first_residual_kernel(
    lam, s0, s1, s2, s3, qa, qb, qc, qd, c_high, c_low, source_q, source_c, quarter, slots, scr
):
    me = lax.axis_index("col")
    for step, s in zip(team_steps, (s0, s1, s2, s3)):
        scr[source_of(me, step)] = s[0:ALLC, :]
    residual_of(lam, scr, (qa, qb, qc, qd), c_high, c_low, source_q, source_c, quarter, slots)


def dot_pair(x, w):
    x_high, x_low = split(x)
    w_high, w_low = split(w)
    return dot(x_high, w_high) + (dot(x_low, w_high) + dot(x_high, w_low))


def residual_kernel(
    lam, s0, s1, s2, s3, qa, qb, qc, qd, c_high, c_low, source_q, source_c,
    modes, margin_modes, near, quarter, slots, out, scr, rhs,
):
    me = lax.axis_index("col")
    for step, s in zip(team_steps, (s0, s1, s2, s3)):
        pair = s[ALLC:, :]
        rhs[source_of(me, step), 0:32, :] = pair
        rhs[source_of(me, step), 32:64, :] = pltpu.roll(pair, 64, 1)
        scr[source_of(me, step)] = s[0:ALLC, :]
    coarse = dot_pair(near[...].reshape(40, 256), rhs[...].reshape(256, 128))
    coarse = jnp.concatenate([coarse, jnp.zeros((88, 128), f32)], axis=0).T[:ALLC]

    def lift(number, shape):
        return damping * dot_pair(coarse[:, 8 * number : 8 * number + 8], shape)

    for b in range(4):
        scr[b] = scr[b] + lift(b, margin_modes[b])
    for b in range(3):
        to = slice(BLOCK * b, BLOCK * b + BLOCK)
        out[:, to] = lam[:, to] + lift(4, modes[:, to])
    residual_of(out, scr, (qa, qb, qc, qd), c_high, c_low, source_q, source_c, quarter, slots)


def residual_join_kernel(quarter, got, out):
    out[:, 0:QUART] = quarter[...]
    out[:, QUART:] = got[...]


def solve_kernel(x0, x1, x2, x3, high, low, m_high, m_low, modes, solved, send_a, send_b, message, scr):
    me = lax.axis_index("col")
    for step, x in zip(team_steps, (x0, x1, x2, x3)):
        scr[source_of(me, step)] = x[...]
    total = jnp.zeros((ALLC, BLOCK), f32)
    extra = jnp.zeros((ALLC, SLOT), f32)
    rhs = jnp.zeros((8, ALLC), f32)
    for b in range(4):
        x = scr[b]
        extra = extra + dot3(x, m_high[b], m_low[b])
        total = total + dot3(x, high[b], low[b])
        rhs = rhs + lax.dot_general(
            modes[:, QUART * b : QUART * b + QUART],
            x[:, :QUART],
            contract_last,
            precision=highest,
            preferred_element_type=f32,
        )
    rhs = jnp.concatenate([rhs, jnp.zeros((8, 128 - ALLC), f32)], axis=1)
    below = jnp.concatenate([rhs, jnp.zeros((ALLC - 8, 128), f32)], axis=0)
    solved[...] = total
    send_a[...] = jnp.where(me == 3, total[:, 3 * SLOT :], extra)
    send_b[...] = jnp.where(me == 3, total[:, SLOT : 2 * SLOT], below)
    message[...] = rhs


def coarse_part(inverse, coarse_rhs):
    coarse = jnp.dot(inverse[...], coarse_rhs[...], precision=highest, preferred_element_type=f32)
    return coarse.T


def field_part(lam, solved, back, spread, coarse, modes):
    lifted = jnp.dot(coarse, modes, precision=highest, preferred_element_type=f32)
    return lam + damping * (solved + dot2(back, spread) + lifted)


def entries_kernel(message, everyone):
    everyone[...] = jnp.broadcast_to(message[...][None], everyone.shape)


def solve_join_kernel(solved, got_a, got_b, message, odd, out):
    first = lax.axis_index("col") == 0
    out[0:ALLC, 0:BLOCK] = solved[...]
    out[0:ALLC, BLOCK:] = jnp.where(first, got_b[...], got_a[...])
    out[ALLC:, :] = jnp.zeros((8, PART), f32)
    out[ALLC : ALLC + MODES, 0:128] = jnp.where(first, message[0:MODES, :], got_b[0:MODES, :])
    out[ALLC + MODES : ALLC + 8, 0:128] = odd[0:MODES, :]


def final_join_kernel(solved, got_a, got_b, p0, p1, p2, p3, scr):
    me = lax.axis_index("col")
    scr[:, 0:BLOCK] = solved[...]
    scr[:, BLOCK:] = jnp.where(me == 0, got_b[...], got_a[...])
    for step, p in enumerate((p0, p1, p2, p3)):
        p[...] = scr[pl.ds(pl.multiple_of(COLS * lax.rem(me + step, TEAM), COLS), COLS), :]


def update_kernel(x0, x1, x2, x3, lam, spread, pick, out, slots, entries, scr):
    me = lax.axis_index("col")
    for step, x in zip(team_steps, (x0, x1, x2, x3)):
        source = source_of(me, step)
        scr[source] = x[0:ALLC, :]
        entries[pl.ds(pl.multiple_of(8 * source, 8), 8), :] = x[ALLC:, 0:128]
    back = jnp.concatenate([scr[b, :, BLOCK:] for b in margin_holder], axis=1)
    send = jnp.zeros((ALLC, SLOT), f32)
    for b in range(3):
        to = slice(BLOCK * b, BLOCK * b + BLOCK)
        fresh = lam[:, to] + damping * (scr[b, :, :BLOCK] + dot2(back, spread[:, to]))
        out[:, to] = fresh
        send = send + dot2(fresh, pick[to, :])
    slots[...] = send


def update_join_kernel(got, entries, even, odd, out):
    first = lax.axis_index("col") == 0
    out[0:ALLC, :] = got[...]
    left = jnp.where(first, entries[...], even[...])
    place = lax.broadcasted_iota(jnp.int32, left.shape, 1)
    out[ALLC:, :] = jnp.where(place < ALLC, left, pltpu.roll(odd[...], 64, 1))


def final_kernel(x0, x1, x2, x3, lam, spread, modes, inverse, coarse_rhs, out, scr, across):
    me = lax.axis_index("col")
    for step, x in enumerate((x0, x1, x2, x3)):
        scr[source_of(me, step)] = x[...]
    rows = pl.ds(pl.multiple_of(COLS * me, COLS), COLS)
    back = jnp.concatenate([scr[b, :, BLOCK:] for b in margin_holder], axis=1)
    across[...] = coarse_part(inverse, coarse_rhs)
    coarse = across[rows, :]
    for b in range(3):
        to = slice(BLOCK * b, BLOCK * b + BLOCK)
        out[:, to] = field_part(lam[rows, to], scr[b, :, :BLOCK], back, spread[:, to], coarse, modes[:, to])


def call(kernel, outs, scratch, flops, nbytes, *args, after=(), limit=6 << 20):
    taken = len(args)

    def body(*refs):
        kernel(*refs[:taken], *refs[taken + len(after) :])

    return pl.pallas_call(
        body,
        out_shape=[jax.ShapeDtypeStruct(shape, dtype) for shape, dtype in outs],
        in_specs=[pl.BlockSpec(memory_space=pltpu.VMEM)] * taken
        + [pl.BlockSpec(memory_space=pl.ANY)] * len(after),
        out_specs=[pl.BlockSpec(memory_space=pltpu.VMEM)] * len(outs),
        scratch_shapes=[pltpu.VMEM(shape, dtype) for shape, dtype in scratch],
        compiler_params=pltpu.CompilerParams(vmem_limit_bytes=limit),
        cost_estimate=pl.CostEstimate(flops=flops, bytes_accessed=nbytes, transcendentals=0),
        name=kernel.__name__,
    )(*args, *after)


def team_pass(x, sign):
    pairs = []
    for s in range(SUBS):
        for d, step in enumerate(direction_steps):
            t = s + sign * step
            if 0 <= t < SUBS:
                pairs.append((s * TEAM + d, t * TEAM + d))
    return lax.ppermute(x, ("sub", "col"), pairs)


def margin_pass(send_a, send_b, with_coarse):
    first, second = [], []
    for s in range(SUBS):
        for d, source in ((0, 0), (2, 2), (3, 3), (1, 3)):
            t = s + direction_steps[d]
            if 0 <= t < SUBS:
                pair = (s * TEAM + source, t * TEAM + margin_holder[d])
                (second if d == 1 else first).append(pair)
        if with_coarse:
            for c in (1, 2, 3):
                second.append(((s ^ (2 * c)) * TEAM + c - 1, s * TEAM + c))
    axes = ("sub", "col")
    return lax.ppermute(send_a, axes, first), lax.ppermute(send_b, axes, second)


def coarse_pass(x, width, odd):
    pairs = [
        ((s ^ (width * (2 * c + odd))) * TEAM + c, s * TEAM + c)
        for s in range(SUBS)
        for c in range(TEAM)
        if 2 * c + odd > 0
    ]
    return lax.ppermute(x, ("sub", "col"), pairs)


def step_pass(x, step):
    return lax.ppermute(x, "col", [(i, (i + step) % TEAM) for i in range(TEAM)])


def team_share(x):
    return [x] + [step_pass(x, step) for step in team_steps[1:]]


def local(
    adjoint_source,
    start_field,
    row_diagonal,
    row_values,
    row_columns,
    weight_code,
    slot_count,
    slot_rows,
    local_inverse,
    coarse_modes,
    coarse_inverse,
):
    fields, coded = pl.pallas_call(
        opening_kernel,
        out_shape=[jax.ShapeDtypeStruct((2 * COLS, OWN), f32), jax.ShapeDtypeStruct((1, SLOT), f32)],
        in_specs=[pl.BlockSpec(memory_space=pltpu.HBM)] * 4,
        out_specs=[pl.BlockSpec(memory_space=pltpu.VMEM)] * 2,
        scratch_shapes=[
            pltpu.VMEM((1, TEAM), jnp.int32),
            pltpu.VMEM((1, TEAM, SLOT), jnp.int32),
            pltpu.SemaphoreType.DMA((4,)),
        ],
        compiler_params=pltpu.CompilerParams(vmem_limit_bytes=60 << 20),
        cost_estimate=pl.CostEstimate(flops=0, bytes_accessed=400_000, transcendentals=0),
    )(start_field, adjoint_source, slot_count, slot_rows)
    coded = team_pass(coded, 1)
    fields = team_share(fields)
    first = lax.ppermute(local_inverse[0:SLOT], "col", [(3, 0)])
    third = lax.ppermute(local_inverse[2 * SLOT : 3 * SLOT], "col", [(3, 2)])
    diagonal = row_diagonal.reshape(1, OWN)
    code = weight_code.reshape(1, EXT)

    lam, pick, slots = call(
        start_kernel,
        [((ALLC, OWN), f32), ((OWN, SLOT), bf16), ((ALLC + 16, SLOT), f32)],
        [],
        100_000_000,
        1_000_000,
        *fields,
        coded,
        coarse_modes,
        coarse_inverse,
    )
    half = ((EXT // 2, QUART), bf16)
    terms = [((32, QUART), f32), ((32, QUART), jnp.int32)]
    q_pairs = call(
        first_half_kernel,
        [half, half],
        terms,
        3_000_000_000,
        3_000_000,
        row_values,
        row_columns,
        diagonal,
        after=(lam,),
    )
    slots = team_pass(slots, -1)
    (slots,) = call(start_join_kernel, [((ALLC + 24, SLOT), f32)], [], 0, 80_000, slots, coded, after=(q_pairs[0],))
    slots = team_share(slots)
    q_pairs += call(
        second_half_kernel,
        [half, half],
        terms,
        3_000_000_000,
        3_000_000,
        row_values,
        row_columns,
        diagonal,
        after=(slots[0],),
    )
    c_high, c_low = call(
        chosen_kernel,
        [((EXT, SLOT), bf16), ((EXT, SLOT), bf16)],
        [((32, SLOT), f32), ((32, SLOT), jnp.int32), ((80, OWN), f32)],
        2_000_000_000,
        1_000_000,
        row_values,
        row_columns,
        diagonal,
        coded,
        pick,
        after=(slots[0],),
    )
    source_q, source_c, modes, inverse = call(
        source_kernel,
        [((ALLC, QUART), f32), ((ALLC, SLOT), f32), ((8, OWN), f32), ((8, SUBS * 8), f32)],
        [((ALLC, OWN), f32)],
        400_000_000,
        2_000_000,
        *fields,
        pick,
        coarse_modes,
        coarse_inverse,
    )
    w_high, w_low = pl.pallas_call(
        inverse_kernel,
        grid=(4,),
        out_shape=[jax.ShapeDtypeStruct((4, BLOCK, BLOCK), bf16)] * 2,
        in_specs=[
            pl.BlockSpec((BLOCK, QUART), lambda i: (0, i)),
            pl.BlockSpec((BLOCK, SLOT), lambda i: (0, 12 + i)),
            pl.BlockSpec((1, QUART), lambda i: (0, i)),
            pl.BlockSpec((1, SLOT), lambda i: (0, 12 + i)),
        ],
        out_specs=[pl.BlockSpec((1, BLOCK, BLOCK), lambda i: (i, 0, 0))] * 2,
        compiler_params=pltpu.CompilerParams(vmem_limit_bytes=12 << 20),
        cost_estimate=pl.CostEstimate(flops=4_000_000_000, bytes_accessed=8_000_000, transcendentals=0),
    )(local_inverse, local_inverse, code, code)
    m_high, m_low = call(
        margin_kernel,
        [((4, BLOCK, SLOT), bf16), ((4, BLOCK, SLOT), bf16)],
        [],
        1_000_000_000,
        3_000_000,
        first,
        third,
        code,
    )

    small = 600_000_000
    piece = ((ALLC, SLOT), f32)
    for iteration in range(ITERS):
        last = iteration == ITERS - 1
        operator = (*q_pairs, c_high, c_low, source_q, source_c)
        if iteration == 0:
            quarter, send = call(
                first_residual_kernel,
                [((ALLC, QUART), f32), piece],
                [((4, ALLC, SLOT), f32)],
                small,
                5_000_000,
                lam,
                *slots,
                *operator,
            )
            spread, margin_modes, near = call(
                lists_kernel,
                [((BLOCK, OWN), bf16), ((4, 8, SLOT), f32), ((5, 8, 256), f32)],
                [],
                10_000_000,
                2_000_000,
                *slots,
                coarse_inverse,
            )
        else:
            quarter, send, lam = call(
                residual_kernel,
                [((ALLC, QUART), f32), piece, ((ALLC, OWN), f32)],
                [((4, ALLC, SLOT), f32), ((4, ALLC, 128), f32)],
                small,
                5_000_000,
                lam,
                *slots,
                *operator,
                modes,
                margin_modes,
                near,
            )
        (block,) = call(
            residual_join_kernel, [((ALLC, BLOCK), f32)], [], 0, 260_000, quarter, team_pass(send, -1)
        )
        blocks = team_share(block)
        solved, send_a, send_b, message = call(
            solve_kernel,
            [((ALLC, BLOCK), f32), piece, piece, ((8, 128), f32)],
            [((4, ALLC, BLOCK), f32)],
            small,
            5_000_000,
            *blocks,
            w_high,
            w_low,
            m_high,
            m_low,
            modes,
        )
        got = margin_pass(send_a, send_b, not last)
        if not last:
            odd = coarse_pass(message, 1, 1)
            (part,) = call(
                solve_join_kernel, [((ALLC + 8, PART), f32)], [], 0, 400_000, solved, *got, message, odd
            )
            lam, send, entries = call(
                update_kernel,
                [((ALLC, OWN), f32), piece, ((32, 128), f32)],
                [((4, ALLC, PART), f32)],
                small,
                3_000_000,
                *team_share(part),
                lam,
                spread,
                pick,
            )
            send = team_pass(send, -1)
            even, odd = coarse_pass(entries, 8, 0), coarse_pass(entries, 8, 1)
            (slots,) = call(
                update_join_kernel, [((ALLC + 32, SLOT), f32)], [], 0, 130_000, send, entries, even, odd
            )
            slots = team_share(slots)
        else:
            (everyone,) = call(
                entries_kernel,
                [((SUBS, 8, 128), f32)],
                [],
                0,
                300_000,
                message,
                after=tuple(got),
            )
            coarse_rhs = lax.all_to_all(everyone, "sub", 0, 0).reshape(SUBS * 8, 128)
            parts = call(
                final_join_kernel,
                [((COLS, PART), f32)] * 4,
                [((ALLC, PART), f32)],
                0,
                400_000,
                solved,
                *got,
            )
            parts = [parts[0]] + [step_pass(parts[step], step) for step in (1, 2, 3)]
            (values,) = call(
                final_kernel,
                [((COLS, OWN), f32)],
                [((4, COLS, PART), f32), ((128, 8), f32)],
                small,
                3_000_000,
                *parts,
                lam,
                spread,
                modes,
                inverse,
                coarse_rhs,
            )
    return values


def solution(mesh):
    return jax.shard_map(
        local,
        mesh=mesh,
        in_specs=(
            P("col", "sub"),
            P("col", "sub"),
            P("sub"),
            P(None, "sub"),
            P(None, "sub"),
            P("sub"),
            P("sub", None),
            P("sub", None, None),
            P(("sub", "col"), None),
            P(None, "sub"),
            P("sub", None),
        ),
        out_specs=P("col", "sub"),
        check_vma=False,
    )
```

```python
import functools
import jax
import jax.numpy as jnp
from jax import lax
from jax.experimental import pallas as pl
from jax.experimental.pallas import tpu as pltpu
from jax.sharding import PartitionSpec as P

ITERS = 3
OWN = 1536
EXT = 2048
SLOT = 128
QUART = 384
BLOCK = 512
PART = 640
TERMS = 26
MODES = 4
SUBS = 64
TEAM = 4
COLS = 16
ALLC = 64

direction_steps = (-2, -1, 1, 2)
damping = 0.7
margin_holder = (1, 0, 2, 3)
team_steps = (0, 1, 3, 2)
highest = lax.Precision.HIGHEST
f32 = jnp.float32
bf16 = jnp.bfloat16
contract_last = (((1,), (1,)), ((), ()))
contract_first = (((0,), (0,)), ((), ()))


def source_of(member, step):
    return lax.rem(member - step + TEAM, TEAM)


def split(x):
    high = x.astype(bf16)
    low = (x - high.astype(f32)).astype(bf16)
    return high, low


def dot(a, b):
    return jnp.dot(a, b, preferred_element_type=f32)


def dot3(x, w_high, w_low):
    rows = x.shape[0]
    high, low = split(x)
    both = dot(jnp.concatenate([high, low], axis=0), w_high)
    return both[:rows] + both[rows:] + dot(high, w_low)


def dot2(x, ones):
    rows = x.shape[0]
    high, low = split(x)
    both = dot(jnp.concatenate([high, low], axis=0), ones)
    return both[:rows] + both[rows:]


def row_list(coded):
    return (coded + 0.5).astype(jnp.int32) - 1


def dot_exact(x, ones):
    rows = x.shape[0]
    high, rest = split(x)
    low = x - high.astype(f32)
    low = (low - rest.astype(f32)).astype(bf16)
    parts = dot(jnp.concatenate([high, rest, low], axis=0), ones)
    return (parts[2 * rows :] + parts[rows : 2 * rows]) + parts[:rows]


def opening_kernel(field, source, count, rows, fields, coded, counts, lists, sems):
    copies = [
        pltpu.make_async_copy(count, counts, sems.at[0]),
        pltpu.make_async_copy(rows, lists, sems.at[1]),
        pltpu.make_async_copy(field, fields.at[0:COLS], sems.at[2]),
        pltpu.make_async_copy(source, fields.at[COLS : 2 * COLS], sems.at[3]),
    ]
    for copy in copies:
        copy.start()
    copies[0].wait()
    copies[1].wait()
    me = lax.axis_index("col")
    place = lax.broadcasted_iota(jnp.int32, (1, TEAM), 1)
    live = jnp.sum(jnp.where(place == me, counts[...], 0), axis=1, keepdims=True)
    index = lax.broadcasted_iota(jnp.int32, (1, SLOT), 1)
    coded[...] = jnp.where(index < live, lists[0, pl.ds(me, 1), :] + 1, 0).astype(f32)
    copies[2].wait()
    copies[3].wait()


def start_kernel(x0, x1, x2, x3, coded, modes, inverse, lam, pick, send):
    me = lax.axis_index("col")
    wanted = row_list(coded[...])
    for step, x in zip(team_steps, (x0, x1, x2, x3)):
        rows = pl.ds(pl.multiple_of(COLS * source_of(me, step), COLS), COLS)
        lam[rows, :] = x[0:COLS, :]
    for n in range(12):
        spot = lax.broadcasted_iota(jnp.int32, (128, SLOT), 0) + 128 * n
        pick[128 * n : 128 * n + 128, :] = (spot == wanted).astype(f32).astype(bf16)
    send[0:ALLC, :] = dot2(lam[...], pick[...])
    send[ALLC : ALLC + MODES, :] = jnp.dot(
        modes[...], pick[...].astype(f32), precision=highest, preferred_element_type=f32
    )
    send[ALLC + MODES : ALLC + 8, :] = jnp.zeros((MODES, SLOT), f32)
    send[ALLC + 8 : ALLC + 8 + MODES, :] = inverse[:, 0:128]
    send[ALLC + 8 + MODES : ALLC + 16, :] = inverse[:, 128:256]


def start_join_kernel(got, coded, out):
    out[0 : ALLC + 16, :] = got[...]
    out[ALLC + 16 :, :] = jnp.broadcast_to(coded[...], (8, SLOT))


def source_kernel(x0, x1, x2, x3, pick, modes, inverse, quarter, chosen, modes_out, inv_out, scr):
    me = lax.axis_index("col")
    for step, x in zip(team_steps, (x0, x1, x2, x3)):
        rows = pl.ds(pl.multiple_of(COLS * source_of(me, step), COLS), COLS)
        scr[rows, :] = x[COLS:, :]
    for j in range(3):
        at = pl.ds(pl.multiple_of(QUART * me + 128 * j, 128), 128)
        quarter[:, 128 * j : 128 * j + 128] = scr[:, at]
    chosen[...] = dot_exact(scr[...], pick[...])
    modes_out[...] = jnp.zeros(modes_out.shape, f32)
    modes_out[0:MODES, :] = modes[...]
    width = SUBS * MODES
    at = lax.broadcasted_iota(jnp.int32, (width, SUBS * 8), 0)
    to = lax.broadcasted_iota(jnp.int32, (width, SUBS * 8), 1)
    spread = jnp.logical_and(at // MODES == to // 8, lax.rem(at, MODES) == lax.rem(to, 8)).astype(f32)
    inv_out[...] = jnp.zeros(inv_out.shape, f32)
    inv_out[0:MODES, :] = jnp.dot(inverse[...], spread, precision=highest, preferred_element_type=f32)


def lists_kernel(s0, s1, s2, s3, inverse, spread, margin_modes, near):
    me = lax.axis_index("col")
    width = SUBS * MODES
    at = lax.broadcasted_iota(jnp.int32, (width, width), 0)
    to = lax.broadcasted_iota(jnp.int32, (width, width), 1)
    other = lax.bitwise_xor(to // MODES, lax.axis_index("sub").astype(jnp.int32))
    turn = (at == MODES * other + lax.rem(to, MODES)).astype(f32)
    near[...] = jnp.zeros(near.shape, f32)

    def turned(left, right):
        return jnp.dot(
            jnp.concatenate([left, right], axis=1), turn, precision=highest, preferred_element_type=f32
        )

    near[4, 0:MODES, :] = turned(inverse[:, 0:128], inverse[:, 128:256])
    for step, s in zip(team_steps, (s0, s1, s2, s3)):
        source = source_of(me, step)
        margin_modes[source] = s[ALLC : ALLC + 8, :]
        near[source, 0:MODES, :] = turned(s[ALLC + 8 : ALLC + 12, :], s[ALLC + 12 : ALLC + 16, :])
        at = pl.multiple_of(SLOT * source, SLOT)
        coded = jnp.concatenate([s[ALLC + 16 :, :], jnp.zeros((120, SLOT), f32)], axis=0).T
        wanted = jnp.broadcast_to(row_list(coded[:, 0:1]), (SLOT, 128))
        for n in range(12):
            spot = lax.broadcasted_iota(jnp.int32, (SLOT, 128), 1) + 128 * n
            spread[pl.ds(at, SLOT), 128 * n : 128 * n + 128] = (spot == wanted).astype(f32).astype(bf16)


def dense(col, val, high, low, lanes, start, tiles):
    def body(number, carry):
        tile = number + start
        b, j = tile // 8, lax.rem(tile // 2, 4)
        first = jnp.where(j < 3, QUART * b + 128 * j, OWN + SLOT * b) + 64 * lax.rem(tile, 2)
        rows = pl.ds(pl.multiple_of(number * 64, 64), 64)
        spot = lax.broadcasted_iota(jnp.int32, (64, 128), 0) + first
        for lane in range(lanes):
            to = slice(128 * lane, 128 * lane + 128)
            total = jnp.zeros((64, 128), f32)
            for term in range(TERMS + 1):
                total = total + jnp.where(spot == col[term : term + 1, to], val[term : term + 1, to], 0.0)
            high[rows, to], low[rows, to] = split(total)
        return carry

    lax.fori_loop(0, tiles, body, 0)


def quarter_terms(values, columns, diagonal, val, col):
    me = lax.axis_index("col")
    for j in range(3):
        at = pl.ds(pl.multiple_of(QUART * me + 128 * j, 128), 128)
        to = slice(128 * j, 128 * j + 128)
        val[0:TERMS, to] = values[:, at]
        col[0:TERMS, to] = columns[:, at]
        val[TERMS : TERMS + 1, to] = diagonal[:, at]
        col[TERMS : TERMS + 1, to] = lax.broadcasted_iota(jnp.int32, (1, 128), 1) + (QUART * me + 128 * j)


def first_half_kernel(values, columns, diagonal, high, low, val, col):
    quarter_terms(values, columns, diagonal, val, col)
    dense(col, val, high, low, 3, 0, 16)


def second_half_kernel(values, columns, diagonal, high, low, val, col):
    quarter_terms(values, columns, diagonal, val, col)
    dense(col, val, high, low, 3, 16, 16)


def chosen_kernel(values, columns, diagonal, coded, pick, high, low, val, col, rows):
    rows[...] = jnp.zeros(rows.shape, f32)
    rows[0:TERMS, :] = values[...]
    rows[32 : 32 + TERMS, :] = columns[...].astype(f32)
    rows[64:65, :] = diagonal[...]
    found = dot_exact(rows[...], pick[...])
    val[0:TERMS, :] = found[0:TERMS]
    col[0:TERMS, :] = (found[32 : 32 + TERMS] + 0.5).astype(jnp.int32)
    val[TERMS : TERMS + 1, :] = found[64:65]
    col[TERMS : TERMS + 1, :] = row_list(coded[...])
    dense(col, val, high, low, 1, 0, 32)


def inverse_kernel(owned, margin, code_owned, code_margin, high, low):
    for j in range(4):
        if j < 3:
            lanes = slice(128 * j, 128 * j + 128)
            tile, code = owned[:, lanes], code_owned[:, lanes]
        else:
            tile, code = margin[...], code_margin[...]
        first, second = split((tile * (1.0 / (1.0 + code.astype(f32)))).T)
        high[0, 128 * j : 128 * j + 128, :] = first
        low[0, 128 * j : 128 * j + 128, :] = second


def residual_of(lam, scr, q_pairs, c_high, c_low, source_q, source_c, quarter, slots):
    owned = jnp.zeros((ALLC, QUART), f32)
    chosen = jnp.zeros((ALLC, SLOT), f32)
    for b in range(4):
        x = jnp.concatenate([lam[:, QUART * b : QUART * b + QUART], scr[b]], axis=1)
        rows = slice(BLOCK * b, BLOCK * b + BLOCK)
        chosen = chosen + dot3(x, c_high[rows, :], c_low[rows, :])
        rows = slice(BLOCK * (b % 2), BLOCK * (b % 2) + BLOCK)
        high, low = q_pairs[2 * (b // 2) : 2 * (b // 2) + 2]
        owned = owned + dot3(x, high[rows, :], low[rows, :])
    quarter[...] = source_q[...] - owned
    slots[...] = source_c[...] - chosen


def margin_kernel(first, third, code_owned, high, low):
    mine = lax.axis_index("col") == 0
    for b in range(4):
        for j in range(4):
            if j < 3:
                n = QUART * b + 128 * j
            else:
                n = OWN + SLOT * b
            lanes = slice(n, n + 128)
            tile = jnp.where(mine, first[:, lanes], third[:, lanes])
            code = code_owned[:, lanes]
            upper, lower = split((tile * (1.0 / (1.0 + code.astype(f32)))).T)
            high[b, 128 * j : 128 * j + 128, :] = upper
            low[b, 128 * j : 128 * j + 128, :] = lower


def first_residual_kernel(
    lam, s0, s1, s2, s3, qa, qb, qc, qd, c_high, c_low, source_q, source_c, quarter, slots, scr
):
    me = lax.axis_index("col")
    for step, s in zip(team_steps, (s0, s1, s2, s3)):
        scr[source_of(me, step)] = s[0:ALLC, :]
    residual_of(lam, scr, (qa, qb, qc, qd), c_high, c_low, source_q, source_c, quarter, slots)


def dot_pair(x, w):
    x_high, x_low = split(x)
    w_high, w_low = split(w)
    return dot(x_high, w_high) + (dot(x_low, w_high) + dot(x_high, w_low))


def residual_kernel(
    lam, s0, s1, s2, s3, qa, qb, qc, qd, c_high, c_low, source_q, source_c,
    modes, margin_modes, near, quarter, slots, out, scr, rhs,
):
    me = lax.axis_index("col")
    for step, s in zip(team_steps, (s0, s1, s2, s3)):
        pair = s[ALLC:, :]
        rhs[source_of(me, step), 0:32, :] = pair
        rhs[source_of(me, step), 32:64, :] = pltpu.roll(pair, 64, 1)
        scr[source_of(me, step)] = s[0:ALLC, :]
    coarse = dot_pair(near[...].reshape(40, 256), rhs[...].reshape(256, 128))
    coarse = jnp.concatenate([coarse, jnp.zeros((88, 128), f32)], axis=0).T[:ALLC]

    def lift(number, shape):
        return damping * dot_pair(coarse[:, 8 * number : 8 * number + 8], shape)

    for b in range(4):
        scr[b] = scr[b] + lift(b, margin_modes[b])
    for b in range(3):
        to = slice(BLOCK * b, BLOCK * b + BLOCK)
        out[:, to] = lam[:, to] + lift(4, modes[:, to])
    residual_of(out, scr, (qa, qb, qc, qd), c_high, c_low, source_q, source_c, quarter, slots)


def residual_join_kernel(quarter, got, out):
    out[:, 0:QUART] = quarter[...]
    out[:, QUART:] = got[...]


def solve_kernel(x0, x1, x2, x3, high, low, m_high, m_low, modes, solved, send_a, send_b, message, scr):
    me = lax.axis_index("col")
    for step, x in zip(team_steps, (x0, x1, x2, x3)):
        scr[source_of(me, step)] = x[...]
    total = jnp.zeros((ALLC, BLOCK), f32)
    extra = jnp.zeros((ALLC, SLOT), f32)
    rhs = jnp.zeros((8, ALLC), f32)
    for b in range(4):
        x = scr[b]
        extra = extra + dot3(x, m_high[b], m_low[b])
        total = total + dot3(x, high[b], low[b])
        m_pair, x_pair = split(modes[:, QUART * b : QUART * b + QUART]), split(x[:, :QUART])
        for one, two in ((0, 0), (0, 1), (1, 0)):
            rhs = rhs + lax.dot_general(m_pair[one], x_pair[two], contract_last, preferred_element_type=f32)
    rhs = jnp.concatenate([rhs, jnp.zeros((8, 128 - ALLC), f32)], axis=1)
    below = jnp.concatenate([rhs, jnp.zeros((ALLC - 8, 128), f32)], axis=0)
    solved[...] = total
    send_a[...] = jnp.where(me == 3, total[:, 3 * SLOT :], extra)
    send_b[...] = jnp.where(me == 3, total[:, SLOT : 2 * SLOT], below)
    message[...] = rhs


def coarse_part(inverse, coarse_rhs):
    coarse = jnp.dot(inverse[...], coarse_rhs[...], precision=highest, preferred_element_type=f32)
    return coarse.T


def field_part(lam, solved, back, spread, coarse, modes):
    lifted = jnp.dot(coarse, modes, precision=highest, preferred_element_type=f32)
    return lam + damping * (solved + dot2(back, spread) + lifted)


def entries_kernel(message, everyone):
    everyone[...] = jnp.broadcast_to(message[...][None], everyone.shape)


def solve_join_kernel(solved, got_a, got_b, message, odd, out):
    first = lax.axis_index("col") == 0
    out[0:ALLC, 0:BLOCK] = solved[...]
    out[0:ALLC, BLOCK:] = jnp.where(first, got_b[...], got_a[...])
    out[ALLC:, :] = jnp.zeros((8, PART), f32)
    out[ALLC : ALLC + MODES, 0:128] = jnp.where(first, message[0:MODES, :], got_b[0:MODES, :])
    out[ALLC + MODES : ALLC + 8, 0:128] = odd[0:MODES, :]


def final_join_kernel(solved, got_a, got_b, p0, p1, p2, p3, scr):
    me = lax.axis_index("col")
    scr[:, 0:BLOCK] = solved[...]
    scr[:, BLOCK:] = jnp.where(me == 0, got_b[...], got_a[...])
    for step, p in enumerate((p0, p1, p2, p3)):
        p[...] = scr[pl.ds(pl.multiple_of(COLS * lax.rem(me + step, TEAM), COLS), COLS), :]


def update_kernel(x0, x1, x2, x3, lam, spread, pick, out, slots, entries, scr):
    me = lax.axis_index("col")
    for step, x in zip(team_steps, (x0, x1, x2, x3)):
        source = source_of(me, step)
        scr[source] = x[0:ALLC, :]
        entries[pl.ds(pl.multiple_of(8 * source, 8), 8), :] = x[ALLC:, 0:128]
    back = jnp.concatenate([scr[b, :, BLOCK:] for b in margin_holder], axis=1)
    send = jnp.zeros((ALLC, SLOT), f32)
    for b in range(3):
        to = slice(BLOCK * b, BLOCK * b + BLOCK)
        fresh = lam[:, to] + damping * (scr[b, :, :BLOCK] + dot2(back, spread[:, to]))
        out[:, to] = fresh
        send = send + dot2(fresh, pick[to, :])
    slots[...] = send


def update_join_kernel(got, entries, even, odd, out):
    first = lax.axis_index("col") == 0
    out[0:ALLC, :] = got[...]
    left = jnp.where(first, entries[...], even[...])
    place = lax.broadcasted_iota(jnp.int32, left.shape, 1)
    out[ALLC:, :] = jnp.where(place < ALLC, left, pltpu.roll(odd[...], 64, 1))


def final_kernel(x0, x1, x2, x3, lam, spread, modes, inverse, coarse_rhs, out, scr, across):
    me = lax.axis_index("col")
    for step, x in enumerate((x0, x1, x2, x3)):
        scr[source_of(me, step)] = x[...]
    rows = pl.ds(pl.multiple_of(COLS * me, COLS), COLS)
    back = jnp.concatenate([scr[b, :, BLOCK:] for b in margin_holder], axis=1)
    across[...] = coarse_part(inverse, coarse_rhs)
    coarse = across[rows, :]
    for b in range(3):
        to = slice(BLOCK * b, BLOCK * b + BLOCK)
        out[:, to] = field_part(lam[rows, to], scr[b, :, :BLOCK], back, spread[:, to], coarse, modes[:, to])


def call(kernel, outs, scratch, flops, nbytes, *args, after=(), limit=6 << 20):
    taken = len(args)

    def body(*refs):
        kernel(*refs[:taken], *refs[taken + len(after) :])

    return pl.pallas_call(
        body,
        out_shape=[jax.ShapeDtypeStruct(shape, dtype) for shape, dtype in outs],
        in_specs=[pl.BlockSpec(memory_space=pltpu.VMEM)] * taken
        + [pl.BlockSpec(memory_space=pl.ANY)] * len(after),
        out_specs=[pl.BlockSpec(memory_space=pltpu.VMEM)] * len(outs),
        scratch_shapes=[pltpu.VMEM(shape, dtype) for shape, dtype in scratch],
        compiler_params=pltpu.CompilerParams(vmem_limit_bytes=limit),
        cost_estimate=pl.CostEstimate(flops=flops, bytes_accessed=nbytes, transcendentals=0),
        name=kernel.__name__,
    )(*args, *after)


def team_pass(x, sign):
    pairs = []
    for s in range(SUBS):
        for d, step in enumerate(direction_steps):
            t = s + sign * step
            if 0 <= t < SUBS:
                pairs.append((s * TEAM + d, t * TEAM + d))
    return lax.ppermute(x, ("sub", "col"), pairs)


def margin_pass(send_a, send_b, with_coarse):
    first, second = [], []
    for s in range(SUBS):
        for d, source in ((0, 0), (2, 2), (3, 3), (1, 3)):
            t = s + direction_steps[d]
            if 0 <= t < SUBS:
                pair = (s * TEAM + source, t * TEAM + margin_holder[d])
                (second if d == 1 else first).append(pair)
        if with_coarse:
            for c in (1, 2, 3):
                second.append(((s ^ (2 * c)) * TEAM + c - 1, s * TEAM + c))
    axes = ("sub", "col")
    return lax.ppermute(send_a, axes, first), lax.ppermute(send_b, axes, second)


def coarse_pass(x, width, odd):
    pairs = [
        ((s ^ (width * (2 * c + odd))) * TEAM + c, s * TEAM + c)
        for s in range(SUBS)
        for c in range(TEAM)
        if 2 * c + odd > 0
    ]
    return lax.ppermute(x, ("sub", "col"), pairs)


def step_pass(x, step):
    return lax.ppermute(x, "col", [(i, (i + step) % TEAM) for i in range(TEAM)])


def team_share(x):
    return [x] + [step_pass(x, step) for step in team_steps[1:]]


def local(
    adjoint_source,
    start_field,
    row_diagonal,
    row_values,
    row_columns,
    weight_code,
    slot_count,
    slot_rows,
    local_inverse,
    coarse_modes,
    coarse_inverse,
):
    fields, coded = pl.pallas_call(
        opening_kernel,
        out_shape=[jax.ShapeDtypeStruct((2 * COLS, OWN), f32), jax.ShapeDtypeStruct((1, SLOT), f32)],
        in_specs=[pl.BlockSpec(memory_space=pltpu.HBM)] * 4,
        out_specs=[pl.BlockSpec(memory_space=pltpu.VMEM)] * 2,
        scratch_shapes=[
            pltpu.VMEM((1, TEAM), jnp.int32),
            pltpu.VMEM((1, TEAM, SLOT), jnp.int32),
            pltpu.SemaphoreType.DMA((4,)),
        ],
        compiler_params=pltpu.CompilerParams(vmem_limit_bytes=60 << 20),
        cost_estimate=pl.CostEstimate(flops=0, bytes_accessed=400_000, transcendentals=0),
    )(start_field, adjoint_source, slot_count, slot_rows)
    coded = team_pass(coded, 1)
    fields = team_share(fields)
    first = lax.ppermute(local_inverse[0:SLOT], "col", [(3, 0)])
    third = lax.ppermute(local_inverse[2 * SLOT : 3 * SLOT], "col", [(3, 2)])
    diagonal = row_diagonal.reshape(1, OWN)
    code = weight_code.reshape(1, EXT)

    lam, pick, slots = call(
        start_kernel,
        [((ALLC, OWN), f32), ((OWN, SLOT), bf16), ((ALLC + 16, SLOT), f32)],
        [],
        100_000_000,
        1_000_000,
        *fields,
        coded,
        coarse_modes,
        coarse_inverse,
    )
    half = ((EXT // 2, QUART), bf16)
    terms = [((32, QUART), f32), ((32, QUART), jnp.int32)]
    q_pairs = call(
        first_half_kernel,
        [half, half],
        terms,
        3_000_000_000,
        3_000_000,
        row_values,
        row_columns,
        diagonal,
        after=(lam,),
    )
    slots = team_pass(slots, -1)
    (slots,) = call(start_join_kernel, [((ALLC + 24, SLOT), f32)], [], 0, 80_000, slots, coded, after=(q_pairs[0],))
    slots = team_share(slots)
    q_pairs += call(
        second_half_kernel,
        [half, half],
        terms,
        3_000_000_000,
        3_000_000,
        row_values,
        row_columns,
        diagonal,
        after=(slots[0],),
    )
    c_high, c_low = call(
        chosen_kernel,
        [((EXT, SLOT), bf16), ((EXT, SLOT), bf16)],
        [((32, SLOT), f32), ((32, SLOT), jnp.int32), ((80, OWN), f32)],
        2_000_000_000,
        1_000_000,
        row_values,
        row_columns,
        diagonal,
        coded,
        pick,
        after=(slots[0],),
    )
    source_q, source_c, modes, inverse = call(
        source_kernel,
        [((ALLC, QUART), f32), ((ALLC, SLOT), f32), ((8, OWN), f32), ((8, SUBS * 8), f32)],
        [((ALLC, OWN), f32)],
        400_000_000,
        2_000_000,
        *fields,
        pick,
        coarse_modes,
        coarse_inverse,
    )
    w_high, w_low = pl.pallas_call(
        inverse_kernel,
        grid=(4,),
        out_shape=[jax.ShapeDtypeStruct((4, BLOCK, BLOCK), bf16)] * 2,
        in_specs=[
            pl.BlockSpec((BLOCK, QUART), lambda i: (0, i)),
            pl.BlockSpec((BLOCK, SLOT), lambda i: (0, 12 + i)),
            pl.BlockSpec((1, QUART), lambda i: (0, i)),
            pl.BlockSpec((1, SLOT), lambda i: (0, 12 + i)),
        ],
        out_specs=[pl.BlockSpec((1, BLOCK, BLOCK), lambda i: (i, 0, 0))] * 2,
        compiler_params=pltpu.CompilerParams(vmem_limit_bytes=12 << 20),
        cost_estimate=pl.CostEstimate(flops=4_000_000_000, bytes_accessed=8_000_000, transcendentals=0),
    )(local_inverse, local_inverse, code, code)
    m_high, m_low = call(
        margin_kernel,
        [((4, BLOCK, SLOT), bf16), ((4, BLOCK, SLOT), bf16)],
        [],
        1_000_000_000,
        3_000_000,
        first,
        third,
        code,
    )

    small = 600_000_000
    piece = ((ALLC, SLOT), f32)
    for iteration in range(ITERS):
        last = iteration == ITERS - 1
        operator = (*q_pairs, c_high, c_low, source_q, source_c)
        if iteration == 0:
            quarter, send = call(
                first_residual_kernel,
                [((ALLC, QUART), f32), piece],
                [((4, ALLC, SLOT), f32)],
                small,
                5_000_000,
                lam,
                *slots,
                *operator,
            )
            spread, margin_modes, near = call(
                lists_kernel,
                [((BLOCK, OWN), bf16), ((4, 8, SLOT), f32), ((5, 8, 256), f32)],
                [],
                10_000_000,
                2_000_000,
                *slots,
                coarse_inverse,
            )
        else:
            quarter, send, lam = call(
                residual_kernel,
                [((ALLC, QUART), f32), piece, ((ALLC, OWN), f32)],
                [((4, ALLC, SLOT), f32), ((4, ALLC, 128), f32)],
                small,
                5_000_000,
                lam,
                *slots,
                *operator,
                modes,
                margin_modes,
                near,
            )
        (block,) = call(
            residual_join_kernel, [((ALLC, BLOCK), f32)], [], 0, 260_000, quarter, team_pass(send, -1)
        )
        blocks = team_share(block)
        solved, send_a, send_b, message = call(
            solve_kernel,
            [((ALLC, BLOCK), f32), piece, piece, ((8, 128), f32)],
            [((4, ALLC, BLOCK), f32)],
            small,
            5_000_000,
            *blocks,
            w_high,
            w_low,
            m_high,
            m_low,
            modes,
        )
        got = margin_pass(send_a, send_b, not last)
        if not last:
            odd = coarse_pass(message, 1, 1)
            (part,) = call(
                solve_join_kernel, [((ALLC + 8, PART), f32)], [], 0, 400_000, solved, *got, message, odd
            )
            lam, send, entries = call(
                update_kernel,
                [((ALLC, OWN), f32), piece, ((32, 128), f32)],
                [((4, ALLC, PART), f32)],
                small,
                3_000_000,
                *team_share(part),
                lam,
                spread,
                pick,
            )
            send = team_pass(send, -1)
            even, odd = coarse_pass(entries, 8, 0), coarse_pass(entries, 8, 1)
            (slots,) = call(
                update_join_kernel, [((ALLC + 32, SLOT), f32)], [], 0, 130_000, send, entries, even, odd
            )
            slots = team_share(slots)
        else:
            (everyone,) = call(
                entries_kernel,
                [((SUBS, 8, 128), f32)],
                [],
                0,
                300_000,
                message,
                after=tuple(got),
            )
            coarse_rhs = lax.all_to_all(everyone, "sub", 0, 0).reshape(SUBS * 8, 128)
            parts = call(
                final_join_kernel,
                [((COLS, PART), f32)] * 4,
                [((ALLC, PART), f32)],
                0,
                400_000,
                solved,
                *got,
            )
            parts = [parts[0]] + [step_pass(parts[step], step) for step in (1, 2, 3)]
            (values,) = call(
                final_kernel,
                [((COLS, OWN), f32)],
                [((4, COLS, PART), f32), ((128, 8), f32)],
                small,
                3_000_000,
                *parts,
                lam,
                spread,
                modes,
                inverse,
                coarse_rhs,
            )
    return values


def solution(mesh):
    return jax.shard_map(
        local,
        mesh=mesh,
        in_specs=(
            P("col", "sub"),
            P("col", "sub"),
            P("sub"),
            P(None, "sub"),
            P(None, "sub"),
            P("sub"),
            P("sub", None),
            P("sub", None, None),
            P(("sub", "col"), None),
            P(None, "sub"),
            P("sub", None),
        ),
        out_specs=P("col", "sub"),
        check_vma=False,
    )
```
